256 devices in a mesh: tm: 64 (over y, x_hi, z), dom: 4 (over x_lo, core).
Axes of the slice: x: 4 (x_hi: 2, x_lo: 2; x = x_hi * 2 + x_lo), y: 4, z: 8, core: 2. Of those that a mesh axis runs over, the one named last changes fastest.
Arguments:
- starting_voltage_guess: float32 [1024, 4, 128], P('tm', 'dom'), may hold values from -3 to 3
- injected_amperes: float32 [1024, 4, 128], P('tm', 'dom'), may hold values from -6 to 6
- capacitance: float32 [4, 128], P('dom'), may hold values from 0.5 to 2
- conductance: float32 [4, 128, 128], P('dom'), may hold values from -0.5 to 0.5
- block_pattern: int32 [4, 1, 1], P('dom'), may hold values 0 or 1
- device_gain: float32 [4, 128], P('dom'), may hold values from 0.2 to 2
- link_weight: float32 [4, 128, 128], P('dom'), may hold values from -0.5 to 0.5
- boundary_vertex_list: int32 [4, 128], P('dom'), may hold values from 0 to 127, as said below
- diagonal_reciprocals: float32 [1024, 4, 1, 128, 128], P('tm', 'dom')
- boundary_jacobian: float32 [4, 128, 128], P('dom'), may hold values from -6 to 6
- transfer: float32 [1024, 4, 1, 128, 128], P('tm', 'dom')
Outputs:
- periodic_state: float32 [1024, 4, 128], P('tm', 'dom')
The draws below stay inside these ranges and needn't reach their ends.
Inputs may be any that keep to these rules, and one draw needn't show every extreme that they name: `boundary_vertex_list`: the 128 interface nodes of one partition are distinct.
All inputs are finite; a program needn't handle non-finite values. No bound on the sum of `block_pattern` on one device may be relied on, other than what follows from the above.
Results may differ from the reference program's by a relative error of at most 0.0003.
Values sent between devices are 32-bit elements; how exact they have to be, the bound alone decides.
A program may use at most 64 MiB of HBM per device.

```python
import math
import jax
import jax.numpy as jnp
from jax import lax

BLOCK_WIDTH_NODE = 128
LINKED_NODES = 128
JACOBIAN_TILES = 1
TPD = 16
ITERS = 2
PART_VERTICES = 128
GRID_MOMENTS = 1024
SUBCIRCUITS = 4
N_TM = 64


def identity_operator():
    row_index = lax.broadcasted_iota(jnp.int32, (BLOCK_WIDTH_NODE, BLOCK_WIDTH_NODE), 0)
    col_index = lax.broadcasted_iota(jnp.int32, (BLOCK_WIDTH_NODE, BLOCK_WIDTH_NODE), 1)
    return (row_index == col_index).astype(jnp.float32)


def draw_boundary_vertex_list(key, part):
    keys = jax.random.split(key, SUBCIRCUITS)
    chosen = jax.vmap(lambda single_entry: jax.random.permutation(single_entry, PART_VERTICES)[:LINKED_NODES])(keys)
    return chosen.astype(jnp.int32)


def draw_diagonal_reciprocals(key, part):
    leading_operand = jax.random.fold_in(key, 0)
    perturbation = jax.random.normal(leading_operand, (GRID_MOMENTS, SUBCIRCUITS, JACOBIAN_TILES, BLOCK_WIDTH_NODE, BLOCK_WIDTH_NODE), jnp.float32)
    linear_operator = (identity_operator() + 0.5 * perturbation / math.sqrt(BLOCK_WIDTH_NODE)) * (0.5 / math.sqrt(GRID_MOMENTS))
    return linear_operator


def draw_transfer(key, part):
    leading_operand, trailing_operand, third, power_four_contribution = jax.random.split(key, 4)
    perturbation = jax.random.normal(leading_operand, (GRID_MOMENTS, SUBCIRCUITS, JACOBIAN_TILES, BLOCK_WIDTH_NODE, BLOCK_WIDTH_NODE), jnp.float32)
    mixing = (identity_operator() + 0.1 * perturbation / math.sqrt(BLOCK_WIDTH_NODE)) / math.sqrt(1.01)
    quick_portion = 0.5
    selected = jax.random.uniform(trailing_operand, (SUBCIRCUITS, JACOBIAN_TILES, BLOCK_WIDTH_NODE), jnp.float32)
    gradual_aggregate = jnp.exp(jax.random.uniform(third, (SUBCIRCUITS, JACOBIAN_TILES, BLOCK_WIDTH_NODE), jnp.float32, math.log(0.1), math.log(1.5)))
    slope_readings = jnp.where(selected < quick_portion, 1.0 / 40.0, gradual_aggregate / GRID_MOMENTS)
    orbit_bundles = jax.random.uniform(power_four_contribution, (GRID_MOMENTS,), jnp.float32) < 4.0 / GRID_MOMENTS
    multiplier_pieces = jnp.exp(-slope_readings)[None] * jnp.where(orbit_bundles, 0.65, 1.0)[:, None, None, None]
    return multiplier_pieces[..., None] * mixing


def with_ends(entries, own_key, least, largest):
    longest = entries.shape.index(max(entries.shape))
    spots = []
    for shift in (0, 1):
        where = [jax.random.randint(jax.random.fold_in(own_key, axis), (), 0, length) for axis, length in enumerate(entries.shape)]
        where[longest] = (where[longest] + shift) % entries.shape[longest]
        spots.append(tuple(where))
    return entries.at[spots[0]].set(least).at[spots[1]].set(largest)


def block_scale(own_key, dims, pieces, low, top_value):
    gain = 1.0
    for dim, shards_of in pieces:
        heights = jax.random.uniform(jax.random.fold_in(jax.random.fold_in(own_key, 6), dim), (shards_of,), jnp.float32, low / len(pieces), top_value / len(pieces))
        gain = gain * jnp.repeat(jnp.exp(heights), dims[dim] // shards_of).reshape((-1,) + (1,) * (len(dims) - 1 - dim))
    return gain


def normal_values(own_key, extent, width, bound, cuts=(), held_as=jnp.bfloat16):
    array = jax.random.normal(own_key, extent, jnp.float32) * width
    if len(cuts) > 0:
        array = block_scale(own_key, extent, cuts, -0.22, 0.18) * array
    return jnp.clip(array, min=-bound, max=bound).astype(held_as)


def setup_inputs(seed: int = 0) -> dict:
    splits = jax.random.split(jax.random.key(seed), 12)
    starting_voltage_guess = normal_values(splits[0], (GRID_MOMENTS, SUBCIRCUITS, PART_VERTICES), 0.5, 3.0, ((0, 64), (1, 4)), jnp.float32)
    injected_amperes = normal_values(splits[1], (GRID_MOMENTS, SUBCIRCUITS, PART_VERTICES), 1.0, 6.0, ((0, 64), (1, 4)), jnp.float32)
    capacitance = jnp.clip(jnp.exp(math.log(2.0) - 1.3862944 * jax.random.uniform(splits[2], (SUBCIRCUITS, PART_VERTICES), jnp.float32) ** block_scale(splits[2], (SUBCIRCUITS, PART_VERTICES), ((0, 4),), -0.2, 0.2)), 0.5, 2.0)
    conductance = normal_values(splits[3], (SUBCIRCUITS, PART_VERTICES, PART_VERTICES), PART_VERTICES ** -0.5, 0.5, ((0, 4),), jnp.float32)
    block_pattern = with_ends((jax.random.randint(splits[4], (SUBCIRCUITS, JACOBIAN_TILES, JACOBIAN_TILES), 0, 4) < 3).astype(jnp.int32), jax.random.fold_in(splits[4], 1), 0, 1)
    device_gain = jnp.clip(jnp.exp(math.log(2.0) - 2.3025851 * jax.random.uniform(splits[5], (SUBCIRCUITS, PART_VERTICES), jnp.float32) ** block_scale(splits[5], (SUBCIRCUITS, PART_VERTICES), ((0, 4),), -0.2, 0.2)), 0.2, 2.0)
    link_weight = normal_values(splits[6], (SUBCIRCUITS, PART_VERTICES, LINKED_NODES), LINKED_NODES ** -0.5, 0.5, ((0, 4),), jnp.float32)
    boundary_vertex_list = draw_boundary_vertex_list(jax.random.fold_in(splits[11], 71), 0)
    diagonal_reciprocals = draw_diagonal_reciprocals(jax.random.fold_in(splits[11], 71), 0)
    boundary_jacobian = normal_values(splits[9], (SUBCIRCUITS, PART_VERTICES, LINKED_NODES), (0.8 * GRID_MOMENTS ** 0.5 / LINKED_NODES ** 0.5), 6.0, ((0, 4),), jnp.float32)
    transfer = draw_transfer(jax.random.fold_in(splits[11], 71), 0)
    return dict(starting_voltage_guess=starting_voltage_guess, injected_amperes=injected_amperes, capacitance=capacitance, conductance=conductance, block_pattern=block_pattern, device_gain=device_gain, link_weight=link_weight, boundary_vertex_list=boundary_vertex_list, diagonal_reciprocals=diagonal_reciprocals, boundary_jacobian=boundary_jacobian, transfer=transfer)


EXACT_MODE = lax.Precision.HIGHEST


def linear_map_action(linear_operator, column_array):
    return jnp.einsum('...ij,...j->...i', linear_operator, column_array, precision=EXACT_MODE)


def compose(later_map, earlier_map):
    return jnp.einsum('...ij,...jk->...ik', later_map, earlier_map, precision=EXACT_MODE)


def block_prefix(matrices):
    identity = jnp.broadcast_to(jnp.eye(BLOCK_WIDTH_NODE, dtype=jnp.float32), matrices.shape[1:])

    def forward_step(running, linear_operator):
        running = compose(linear_operator, running)
        return running, running

    def backward_step(running, linear_operator):
        return compose(running, linear_operator), running

    _, prefix = lax.scan(forward_step, identity, matrices)
    _, suffix = lax.scan(backward_step, identity, matrices, reverse=True)
    return prefix, suffix


def periodic_sum(prefix, suffix, matrices, stored_coulombs):
    zero_vector = jnp.zeros(stored_coulombs.shape[1:], jnp.float32)

    def accumulate(running, element):
        linear_operator, column_array = element
        running = linear_map_action(linear_operator, running) + column_array
        return running, running

    _, local_sum = lax.scan(accumulate, zero_vector, (matrices, stored_coulombs))

    def gather_tail(running, element):
        linear_operator, column_array = element
        return running + linear_map_action(linear_operator, column_array), running

    _, tail_sum = lax.scan(gather_tail, zero_vector, (suffix, stored_coulombs), reverse=True)
    whole_map = prefix[-1]
    full_period_sum = local_sum[-1]
    identity = jnp.broadcast_to(jnp.eye(BLOCK_WIDTH_NODE, dtype=jnp.float32), whole_map.shape[1:])
    zero_block = jnp.zeros(full_period_sum.shape[1:], jnp.float32)

    def front_step(running, element):
        map_sofar, sum_sofar = running
        block_map, block_sum = element
        return (compose(block_map, map_sofar), block_sum + linear_map_action(block_map, sum_sofar)), running

    def back_step(running, element):
        map_sofar, sum_sofar = running
        block_map, block_sum = element
        return (compose(map_sofar, block_map), sum_sofar + linear_map_action(map_sofar, block_sum)), running

    _, (front_map, front_sum) = lax.scan(front_step, (identity, zero_block), (whole_map, full_period_sum))
    _, (back_map, back_sum) = lax.scan(back_step, (identity, zero_block), (whole_map, full_period_sum), reverse=True)
    around_map = compose(front_map, back_map)
    around_sum = front_sum + linear_map_action(front_map, back_sum)
    incoming = around_sum[None] + linear_map_action(around_map[None], tail_sum)
    return local_sum + linear_map_action(prefix, incoming)


def carve_submatrix(values):
    reshaped_blocks = values.reshape((N_TM, TPD) + values.shape[1:])
    return jnp.swapaxes(reshaped_blocks, 0, 1)


def reference(starting_voltage_guess, injected_amperes, capacitance, conductance, block_pattern, device_gain, link_weight, boundary_vertex_list, diagonal_reciprocals, boundary_jacobian, transfer):
    expand = jnp.repeat(jnp.repeat(block_pattern, BLOCK_WIDTH_NODE, axis=1), BLOCK_WIDTH_NODE, axis=2).astype(jnp.float32)
    effective = conductance * expand
    matrices = carve_submatrix(transfer)
    prefix, suffix = block_prefix(matrices)
    voltage_profile = starting_voltage_guess
    lookup_position = jnp.broadcast_to(boundary_vertex_list[None], (GRID_MOMENTS, SUBCIRCUITS, LINKED_NODES)).astype(jnp.int32)
    for newton_step in range(ITERS):
        before = jnp.roll(voltage_profile, 1, axis=0)
        outlets = jnp.take_along_axis(voltage_profile, lookup_position, axis=2)
        upstream = jnp.concatenate([jnp.zeros_like(outlets[:, :1]), outlets[:, :-1]], axis=1)
        flows = jnp.einsum('pij,tpj->tpi', effective, voltage_profile, precision=EXACT_MODE)
        linked = jnp.einsum('pik,tpk->tpi', link_weight, upstream, precision=EXACT_MODE)
        residual = capacitance[None] * (voltage_profile - before) + flows + device_gain[None] * jnp.tanh(voltage_profile) - linked - injected_amperes
        entering_current = jnp.zeros((GRID_MOMENTS, LINKED_NODES), jnp.float32)
        solved_parts = []
        for subcircuit in range(SUBCIRCUITS):
            excitation = -residual[:, subcircuit] + jnp.dot(entering_current, boundary_jacobian[subcircuit].T, precision=EXACT_MODE)
            resolved_unknowns = linear_map_action(diagonal_reciprocals[:, subcircuit], excitation.reshape(GRID_MOMENTS, JACOBIAN_TILES, BLOCK_WIDTH_NODE)).reshape(GRID_MOMENTS, PART_VERTICES)
            solved_parts.append(resolved_unknowns)
            entering_current = resolved_unknowns[:, boundary_vertex_list[subcircuit]]
        chord_correction_vector = jnp.stack(solved_parts, axis=1)
        stored_coulombs = carve_submatrix(chord_correction_vector.reshape(GRID_MOMENTS, SUBCIRCUITS, JACOBIAN_TILES, BLOCK_WIDTH_NODE))
        refinement = periodic_sum(prefix, suffix, matrices, stored_coulombs)
        voltage_profile = voltage_profile + jnp.swapaxes(refinement, 0, 1).reshape(GRID_MOMENTS, SUBCIRCUITS, PART_VERTICES)
    return voltage_profile
```

```python
import functools

import jax
import jax.numpy as jnp
from jax import lax
from jax.experimental import pallas as pl
from jax.experimental.pallas import tpu as pltpu
from jax.sharding import PartitionSpec as P

ITERS = 2
F32 = jnp.float32
BF16 = jnp.bfloat16
NN = (((1,), (0,)), ((), ()))
NT = (((1,), (1,)), ((), ()))


def halves(x):
    high = x.astype(BF16)
    return high, (x - high.astype(F32)).astype(BF16)


def product(a, b, dims=NN):
    a_high, a_low = halves(a)
    b_high, b_low = halves(b)
    dot = functools.partial(lax.dot_general, dimension_numbers=dims, preferred_element_type=F32)
    return dot(a_high, b_high) + (dot(a_high, b_low) + dot(a_low, b_high))


def eye(n):
    return lax.broadcasted_iota(jnp.int32, (n, n), 0) == lax.broadcasted_iota(jnp.int32, (n, n), 1)


def as_row(square):
    column = jnp.sum(square, axis=1, keepdims=True)
    return jnp.sum(jnp.where(eye(square.shape[0]), column, 0.0), axis=0, keepdims=True)


def kernel(
    ring, groups, parts, v_ref, inj_ref, cap_ref, cond_ref, pat_ref, gain_ref, lw_ref, bvl_ref, dinv_ref, bj_ref, tr_ref,
    out_ref, pair2, pair4, pair8, pre, suf, coup, links_t, whole, sufrel, vmat, umat, gwhole, fz, acc,
    before_in, bvl_in, up_in, corr_in, corr, vnext, local, tails, bvec, bsum,
    send_sem, whole_sem, gwhole_sem, bvec_sem, bsum_sem, small_sem, up_sem, corr_sem,
):
    points, nodes = v_ref.shape
    tm, part = lax.axis_index("tm"), lax.axis_index("dom")
    count = ring * groups
    z, g = lax.rem(tm, ring), lax.div(tm, ring)

    def ring_peer(m):
        return g * ring + lax.rem(z + m, ring)

    def group_peer(m):
        return lax.rem(g + m, groups) * ring + z

    barrier = pltpu.get_barrier_semaphore()
    for m in range(1, ring):
        pl.semaphore_signal(barrier, inc=1, device_id={"tm": ring_peer(m)})
    for m in range(1, groups):
        pl.semaphore_signal(barrier, inc=1, device_id={"tm": group_peer(m)})
    for step in (1, count - 1):
        pl.semaphore_signal(barrier, inc=1, device_id={"tm": lax.rem(tm + step, count)})
    for step in (1, parts - 1):
        pl.semaphore_signal(barrier, inc=1, device_id={"dom": lax.rem(part + step, parts)})

    identity = jnp.where(eye(nodes), 1.0, 0.0)

    for source, target in ((tr_ref, pair2), (pair2, pair4), (pair4, pair8)):
        length = target.shape[0]
        inner = min(4, length)

        @pl.loop(0, length // inner)
        def _(k):
            for i in range(inner):
                e = k * inner + i
                target[e] = product(source[2 * e + 1], source[2 * e])

    whole[0] = product(pair8[1], pair8[0])

    pl.semaphore_wait(barrier, ring - 1 + groups - 1 + 4)

    started = []

    def send(source, target, index, sem, **where):
        copy = pltpu.make_async_remote_copy(
            src_ref=source, dst_ref=target, send_sem=send_sem.at[index], recv_sem=sem,
            device_id=where, device_id_type=pl.DeviceIdType.MESH,
        )
        return copy

    index = iter(range(1000))

    def start(source, target, sem, **where):
        copy = send(source, target, next(index), sem, **where)
        copy.start()
        started.append(copy)
        return copy

    to_next = []

    def start_next(source, target, sem):
        copy = send(source, target, next(index), sem, dom=lax.rem(part + 1, parts))

        @pl.when(part < parts - 1)
        def _():
            copy.start()

        to_next.append(copy)
        return copy

    before_copy = start(v_ref.at[points - 1 :], before_in, small_sem.at[0], tm=lax.rem(tm + 1, count))
    bvl_copy = start_next(bvl_ref, bvl_in, small_sem.at[1])
    up_copies = [start_next(v_ref, up_in.at[0], up_sem.at[0])]
    whole_copies = [
        start(whole.at[0], whole.at[m], whole_sem.at[m], tm=ring_peer(m)) for m in range(1, ring)
    ]

    pre[0] = tr_ref[0]
    pre[1] = pair2[0]
    pre[3] = pair4[0]
    pre[7] = pair8[0]
    pre[15] = whole[0]
    pre[5] = product(pair2[2], pair4[0])
    pre[9] = product(pair2[4], pair8[0])
    pre[11] = product(pair4[2], pair8[0])
    pre[13] = product(pair2[6], pre[11])
    suf[15] = identity
    suf[14] = tr_ref[15]
    suf[13] = pair2[7]
    suf[11] = pair4[3]
    suf[7] = pair8[1]
    suf[9] = product(pair4[3], pair2[5])
    suf[5] = product(pair8[1], pair2[3])
    suf[3] = product(pair8[1], pair4[1])
    suf[1] = product(suf[3], pair2[1])

    @pl.loop(0, 7)
    def _(k):
        pre[2 * k + 2] = product(tr_ref[2 * k + 2], pre[2 * k + 1])
        suf[2 * k] = product(suf[2 * k + 1], tr_ref[2 * k + 1])

    @pl.when(part > 0)
    def _():
        bvl_copy.wait_recv()
        row = lax.broadcasted_iota(jnp.int32, (nodes, nodes), 0)
        spread = jnp.where(row == bvl_in[...], 1.0, 0.0)
        links_t[...] = product(spread, lw_ref[...], NT)
        acc[0:nodes] = product(bj_ref[...], spread, NT)

        @pl.loop(0, points // 2)
        def _(k):
            for i in range(2):
                coup[2 * k + i] = product(dinv_ref[2 * k + i], acc[0:nodes])

    effective = cond_ref[...] * pat_ref[0, 0].astype(F32)

    def residual(v, before, it):
        r = (
            inj_ref[...]
            - cap_ref[...] * (v - before)
            - product(v, effective, NT)
            - gain_ref[...] * jnp.tanh(v)
        )
        local[...] = r

        @pl.when(part > 0)
        def _():
            up_copies[it].wait_recv()
            local[...] = local[...] + product(up_in[it], links_t[...])

    def act_each(matrices, vectors, store):
        @pl.loop(0, points // 4)
        def _(k):
            for i in range(4):
                t = 4 * k + i
                store(t, as_row(matrices[t] * vectors[pl.ds(t, 1), :]))

    corr_copies = []

    def correct(it):
        def put(t, row):
            corr[it, pl.ds(t, 1), :] = row

        def add(t, row):
            corr[it, pl.ds(t, 1), :] = corr[it, pl.ds(t, 1), :] + row

        act_each(dinv_ref, local, put)
        corr_copies.append(
            send(corr.at[it], corr_in.at[it], next(index), corr_sem.at[it], dom=lax.rem(part + 1, parts))
        )

        @pl.when(part > 0)
        def _():
            corr_copies[it].wait_recv()
            act_each(coup, corr_in.at[it], add)

        @pl.when(part < parts - 1)
        def _():
            corr_copies[it].start()

        total = suf[0] * corr[it, 0:1, :]
        for t in range(1, points):
            total = total + suf[t] * corr[it, t : t + 1, :]
        bvec[it, 0] = as_row(total)
        return [
            start(bvec.at[it, 0], bvec.at[it, m], bvec_sem.at[it, m], tm=ring_peer(m)) for m in range(1, ring)
        ]

    def sum_local(it):
        def step(t, x):
            x = as_row(tr_ref[t] * x) + corr[it, pl.ds(t, 1), :]
            local[pl.ds(t, 1), :] = x
            return x

        lax.fori_loop(0, points, step, jnp.zeros((1, nodes), F32))

        def put(t, row):
            tails[pl.ds(t, 1), :] = row

        act_each(suf, corr.at[it], put)
        running = jnp.zeros((1, nodes), F32)
        for t in range(points - 1, -1, -1):
            own = tails[t : t + 1, :]
            tails[t : t + 1, :] = running
            running = running + own

    def sum_ring(it, copies):
        total = sufrel[0] * bvec[it, 0]
        for m in range(1, ring):
            copies[m - 1].wait_recv()
            total = total + sufrel[m] * bvec[it, m]
        bsum[it, 0] = as_row(total)
        return [
            start(bsum.at[it, 0], bsum.at[it, m], bsum_sem.at[it, m], tm=group_peer(m)) for m in range(1, groups)
        ]

    def close(it, copies, v, store):
        near = umat[1] * bvec[it, 1]
        for m in range(2, ring):
            near = near + umat[m] * bvec[it, m]
        wrapped = product(jnp.concatenate([tails[...], jnp.broadcast_to(bvec[it, 0], (8, nodes))], axis=0), umat[0], NT)
        near = near
        for m in range(1, groups):
            copies[m - 1].wait_recv()
            near = near + fz[m - 1] * bsum[it, m]
        entering = wrapped + as_row(near)
        tails[...] = entering[0:points]

        def put(t, row):
            store(t, v[pl.ds(t, 1), :] + local[pl.ds(t, 1), :] + row)

        act_each(pre, tails, put)
        return entering[points : points + 1]

    v0 = v_ref[...]
    before_copy.wait_recv()
    residual(v0, jnp.concatenate([before_in[...], v0[: points - 1]], axis=0), 0)
    ring_copies = correct(0)
    sum_local(0)

    for copy in whole_copies:
        copy.wait_recv()
    acc[0:nodes] = identity
    acc[nodes:] = identity

    def ring_step(k, _):
        j = ring - 1 - k
        m = lax.rem(z - j + ring, ring)
        sufrel[m] = acc[0:nodes]
        vmat[m] = acc[nodes:]
        new = product(acc[...], whole[m])
        acc[0:nodes] = new[0:nodes]
        acc[nodes:] = jnp.where(j < z, new[nodes:], acc[nodes:])
        return 0

    lax.fori_loop(0, ring, ring_step, 0)
    gwhole[0] = acc[0:nodes]
    gwhole_copies = [
        start(gwhole.at[0], gwhole.at[m], gwhole_sem.at[m], tm=group_peer(m)) for m in range(1, groups)
    ]
    group_copies = sum_ring(0, ring_copies)

    fz[0] = acc[nodes:]
    for m in range(1, groups):
        gwhole_copies[m - 1].wait_recv()
        fz[m] = product(fz[m - 1], gwhole[m])

    @pl.loop(0, ring // 2)
    def _(k):
        for i in range(2):
            m = 2 * k + i
            around = product(fz[groups - 1], sufrel[m])
            umat[m] = jnp.where((m >= 1) & (m <= z), vmat[m], around)

    def put_next(t, row):
        vnext[pl.ds(t, 1), :] = row

    def put_out(t, row):
        out_ref[pl.ds(t, 1), :] = row

    first = close(0, group_copies, v_ref, put_next)
    up_copies.append(start_next(vnext, up_in.at[1], up_sem.at[1]))

    v1 = vnext[...]
    residual(v1, jnp.concatenate([before_in[...] + first, v1[: points - 1]], axis=0), 1)
    ring_copies = correct(1)
    sum_local(1)
    group_copies = sum_ring(1, ring_copies)
    close(1, group_copies, vnext, put_out)

    for copy in started:
        copy.wait_send()

    @pl.when(part < parts - 1)
    def _():
        for copy in to_next + corr_copies:
            copy.wait_send()


def per_device(
    starting_voltage_guess,
    injected_amperes,
    capacitance,
    conductance,
    block_pattern,
    device_gain,
    link_weight,
    boundary_vertex_list,
    diagonal_reciprocals,
    boundary_jacobian,
    transfer,
    ring,
):
    points, _, nodes = starting_voltage_guess.shape
    count, parts = lax.axis_size("tm"), lax.axis_size("dom")
    groups = count // ring
    square = (nodes, nodes)
    vmem = pl.BlockSpec(memory_space=pltpu.VMEM)
    smem = pl.BlockSpec(memory_space=pltpu.SMEM)
    scratch = [
        pltpu.VMEM((points // 2,) + square, F32),
        pltpu.VMEM((points // 4,) + square, F32),
        pltpu.VMEM((points // 8,) + square, F32),
        pltpu.VMEM((points,) + square, F32),
        pltpu.VMEM((points,) + square, F32),
        pltpu.VMEM((points,) + square, F32),
        pltpu.VMEM(square, F32),
        pltpu.VMEM((ring,) + square, F32),
        pltpu.VMEM((ring,) + square, F32),
        pltpu.VMEM((ring,) + square, F32),
        pltpu.VMEM((ring,) + square, F32),
        pltpu.VMEM((groups,) + square, F32),
        pltpu.VMEM((groups,) + square, F32),
        pltpu.VMEM((2 * nodes, nodes), F32),
        pltpu.VMEM((1, nodes), F32),
        pltpu.VMEM((1, nodes), jnp.int32),
        pltpu.VMEM((ITERS, points, nodes), F32),
        pltpu.VMEM((ITERS, points, nodes), F32),
        pltpu.VMEM((ITERS, points, nodes), F32),
        pltpu.VMEM((points, nodes), F32),
        pltpu.VMEM((points, nodes), F32),
        pltpu.VMEM((points, nodes), F32),
        pltpu.VMEM((ITERS, ring, 1, nodes), F32),
        pltpu.VMEM((ITERS, groups, 1, nodes), F32),
        pltpu.SemaphoreType.DMA((3 + ITERS * 2 + 3 * (ring + groups),)),
        pltpu.SemaphoreType.DMA((ring,)),
        pltpu.SemaphoreType.DMA((groups,)),
        pltpu.SemaphoreType.DMA((ITERS, ring)),
        pltpu.SemaphoreType.DMA((ITERS, groups)),
        pltpu.SemaphoreType.DMA((2,)),
        pltpu.SemaphoreType.DMA((ITERS,)),
        pltpu.SemaphoreType.DMA((ITERS,)),
    ]
    out = pl.pallas_call(
        functools.partial(kernel, ring, groups, parts),
        out_shape=jax.ShapeDtypeStruct((points, nodes), F32),
        in_specs=[vmem] * 4 + [smem] + [vmem] * 6,
        out_specs=vmem,
        scratch_shapes=scratch,
        compiler_params=pltpu.CompilerParams(
            collective_id=0, has_side_effects=True, vmem_limit_bytes=48 * 1024 * 1024
        ),
        name="newton",
    )(
        starting_voltage_guess[:, 0],
        injected_amperes[:, 0],
        capacitance,
        conductance[0],
        block_pattern[0],
        device_gain,
        link_weight[0],
        boundary_vertex_list,
        diagonal_reciprocals[:, 0, 0],
        boundary_jacobian[0],
        transfer[:, 0, 0],
    )
    return out[:, None]


def solution(mesh):
    in_specs = (
        P("tm", "dom", None),
        P("tm", "dom", None),
        P("dom", None),
        P("dom", None, None),
        P("dom", None, None),
        P("dom", None),
        P("dom", None, None),
        P("dom", None),
        P("tm", "dom", None, None, None),
        P("dom", None, None),
        P("tm", "dom", None, None, None),
    )
    out_specs = P("tm", "dom", None)
    count = mesh.shape["tm"]
    ring = 8 if count >= 64 else 2
    return jax.shard_map(
        functools.partial(per_device, ring=ring), mesh=mesh, in_specs=in_specs, out_specs=out_specs, check_vma=False
    )
```

```python
import functools

import jax
import jax.numpy as jnp
from jax import lax
from jax.experimental import pallas as pl
from jax.experimental.pallas import tpu as pltpu
from jax.sharding import PartitionSpec as P

ITERS = 2
F32 = jnp.float32
BF16 = jnp.bfloat16
NN = (((1,), (0,)), ((), ()))
NT = (((1,), (1,)), ((), ()))


def halves(x):
    high = x.astype(BF16)
    return high, (x - high.astype(F32)).astype(BF16)


def product(a, b, dims=NN):
    a_high, a_low = halves(a)
    b_high, b_low = halves(b)
    dot = functools.partial(lax.dot_general, dimension_numbers=dims, preferred_element_type=F32)
    return dot(a_high, b_high) + (dot(a_high, b_low) + dot(a_low, b_high))


def eye(n):
    return lax.broadcasted_iota(jnp.int32, (n, n), 0) == lax.broadcasted_iota(jnp.int32, (n, n), 1)


def as_row(square):
    column = jnp.sum(square, axis=1, keepdims=True)
    return jnp.sum(jnp.where(eye(square.shape[0]), column, 0.0), axis=0, keepdims=True)


def kernel(
    ring, groups, parts, v_hbm, inj_hbm, cap_hbm, cond_hbm, pat_hbm, gain_hbm, lw_hbm, bvl_hbm, dinv_hbm, bj_hbm, tr_hbm,
    out_ref, v_ref, inj_ref, cap_ref, cond_ref, pat_ref, gain_ref, lw_ref, bvl_ref, dinv_ref, bj_ref, tr_ref, pair2, pair4, pair8, pre, suf, coup, links_t, whole, sufrel, vmat, umat, gwhole, fz, acc,
    before_in, bvl_in, up_in, corr_in, corr, vnext, local, tails, bvec, bsum,
    load_sem, send_sem, whole_sem, gwhole_sem, bvec_sem, bsum_sem, small_sem, up_sem, corr_sem,
):
    points, nodes = v_ref.shape
    tm, part = lax.axis_index("tm"), lax.axis_index("dom")
    count = ring * groups
    z, g = lax.rem(tm, ring), lax.div(tm, ring)

    def ring_peer(m):
        return g * ring + lax.rem(z + m, ring)

    def group_peer(m):
        return lax.rem(g + m, groups) * ring + z

    loads = {}
    for name, source, target in (
        ("tr", tr_hbm, tr_ref), ("v", v_hbm, v_ref), ("bvl", bvl_hbm, bvl_ref), ("lw", lw_hbm, lw_ref),
        ("bj", bj_hbm, bj_ref), ("dinv", dinv_hbm, dinv_ref), ("inj", inj_hbm, inj_ref), ("cap", cap_hbm, cap_ref),
        ("cond", cond_hbm, cond_ref), ("gain", gain_hbm, gain_ref), ("pat", pat_hbm, pat_ref),
    ):
        loads[name] = pltpu.make_async_copy(source, target, load_sem.at[len(loads)])
        loads[name].start()

    barrier = pltpu.get_barrier_semaphore()
    for m in range(1, ring):
        pl.semaphore_signal(barrier, inc=1, device_id={"tm": ring_peer(m)})
    for m in range(1, groups):
        pl.semaphore_signal(barrier, inc=1, device_id={"tm": group_peer(m)})
    for step in (1, count - 1):
        pl.semaphore_signal(barrier, inc=1, device_id={"tm": lax.rem(tm + step, count)})
    for step in (1, parts - 1):
        pl.semaphore_signal(barrier, inc=1, device_id={"dom": lax.rem(part + step, parts)})

    identity = jnp.where(eye(nodes), 1.0, 0.0)

    loads["tr"].wait()

    for source, target in ((tr_ref, pair2), (pair2, pair4), (pair4, pair8)):
        length = target.shape[0]
        inner = min(4, length)

        @pl.loop(0, length // inner)
        def _(k):
            for i in range(inner):
                e = k * inner + i
                target[e] = product(source[2 * e + 1], source[2 * e])

    whole[0] = product(pair8[1], pair8[0])

    for name in loads:
        if name != "tr":
            loads[name].wait()
    pl.semaphore_wait(barrier, ring - 1 + groups - 1 + 4)

    started = []

    def send(source, target, index, sem, **where):
        copy = pltpu.make_async_remote_copy(
            src_ref=source, dst_ref=target, send_sem=send_sem.at[index], recv_sem=sem,
            device_id=where, device_id_type=pl.DeviceIdType.MESH,
        )
        return copy

    index = iter(range(1000))

    def start(source, target, sem, **where):
        copy = send(source, target, next(index), sem, **where)
        copy.start()
        started.append(copy)
        return copy

    to_next = []

    def start_next(source, target, sem):
        copy = send(source, target, next(index), sem, dom=lax.rem(part + 1, parts))

        @pl.when(part < parts - 1)
        def _():
            copy.start()

        to_next.append(copy)
        return copy

    before_copy = start(v_ref.at[points - 1 :], before_in, small_sem.at[0], tm=lax.rem(tm + 1, count))
    bvl_copy = start_next(bvl_ref, bvl_in, small_sem.at[1])
    up_copies = [start_next(v_ref, up_in.at[0], up_sem.at[0])]
    whole_copies = [
        start(whole.at[0], whole.at[m], whole_sem.at[m], tm=ring_peer(m)) for m in range(1, ring)
    ]

    pre[0] = tr_ref[0]
    pre[1] = pair2[0]
    pre[3] = pair4[0]
    pre[7] = pair8[0]
    pre[15] = whole[0]
    pre[5] = product(pair2[2], pair4[0])
    pre[9] = product(pair2[4], pair8[0])
    pre[11] = product(pair4[2], pair8[0])
    pre[13] = product(pair2[6], pre[11])
    suf[15] = identity
    suf[14] = tr_ref[15]
    suf[13] = pair2[7]
    suf[11] = pair4[3]
    suf[7] = pair8[1]
    suf[9] = product(pair4[3], pair2[5])
    suf[5] = product(pair8[1], pair2[3])
    suf[3] = product(pair8[1], pair4[1])
    suf[1] = product(suf[3], pair2[1])

    @pl.loop(0, 7)
    def _(k):
        pre[2 * k + 2] = product(tr_ref[2 * k + 2], pre[2 * k + 1])
        suf[2 * k] = product(suf[2 * k + 1], tr_ref[2 * k + 1])

    @pl.when(part > 0)
    def _():
        bvl_copy.wait_recv()
        row = lax.broadcasted_iota(jnp.int32, (nodes, nodes), 0)
        spread = jnp.where(row == bvl_in[...], 1.0, 0.0)
        links_t[...] = product(spread, lw_ref[...], NT)
        acc[0:nodes] = product(bj_ref[...], spread, NT)

        @pl.loop(0, points // 2)
        def _(k):
            for i in range(2):
                coup[2 * k + i] = product(dinv_ref[2 * k + i], acc[0:nodes])

    effective = cond_ref[...] * pat_ref[0].astype(F32)

    def residual(v, before, it):
        r = (
            inj_ref[...]
            - cap_ref[...] * (v - before)
            - product(v, effective, NT)
            - gain_ref[...] * jnp.tanh(v)
        )
        local[...] = r

        @pl.when(part > 0)
        def _():
            up_copies[it].wait_recv()
            local[...] = local[...] + product(up_in[it], links_t[...])

    def act_each(matrices, vectors, store):
        @pl.loop(0, points // 4)
        def _(k):
            for i in range(4):
                t = 4 * k + i
                store(t, as_row(matrices[t] * vectors[pl.ds(t, 1), :]))

    corr_copies = []

    def correct(it):
        def put(t, row):
            corr[it, pl.ds(t, 1), :] = row

        def add(t, row):
            corr[it, pl.ds(t, 1), :] = corr[it, pl.ds(t, 1), :] + row

        act_each(dinv_ref, local, put)
        corr_copies.append(
            send(corr.at[it], corr_in.at[it], next(index), corr_sem.at[it], dom=lax.rem(part + 1, parts))
        )

        @pl.when(part > 0)
        def _():
            corr_copies[it].wait_recv()
            act_each(coup, corr_in.at[it], add)

        @pl.when(part < parts - 1)
        def _():
            corr_copies[it].start()

        total = suf[0] * corr[it, 0:1, :]
        for t in range(1, points):
            total = total + suf[t] * corr[it, t : t + 1, :]
        bvec[it, 0] = as_row(total)
        return [
            start(bvec.at[it, 0], bvec.at[it, m], bvec_sem.at[it, m], tm=ring_peer(m)) for m in range(1, ring)
        ]

    def sum_local(it):
        def step(t, x):
            x = as_row(tr_ref[t] * x) + corr[it, pl.ds(t, 1), :]
            local[pl.ds(t, 1), :] = x
            return x

        lax.fori_loop(0, points, step, jnp.zeros((1, nodes), F32))

        def put(t, row):
            tails[pl.ds(t, 1), :] = row

        act_each(suf, corr.at[it], put)
        running = jnp.zeros((1, nodes), F32)
        for t in range(points - 1, -1, -1):
            own = tails[t : t + 1, :]
            tails[t : t + 1, :] = running
            running = running + own

    def sum_ring(it, copies):
        total = sufrel[0] * bvec[it, 0]
        for m in range(1, ring):
            copies[m - 1].wait_recv()
            total = total + sufrel[m] * bvec[it, m]
        bsum[it, 0] = as_row(total)
        return [
            start(bsum.at[it, 0], bsum.at[it, m], bsum_sem.at[it, m], tm=group_peer(m)) for m in range(1, groups)
        ]

    def close(it, copies, v, store):
        near = umat[1] * bvec[it, 1]
        for m in range(2, ring):
            near = near + umat[m] * bvec[it, m]
        wrapped = product(jnp.concatenate([tails[...], jnp.broadcast_to(bvec[it, 0], (8, nodes))], axis=0), umat[0], NT)
        near = near
        for m in range(1, groups):
            copies[m - 1].wait_recv()
            near = near + fz[m - 1] * bsum[it, m]
        entering = wrapped + as_row(near)
        tails[...] = entering[0:points]

        def put(t, row):
            store(t, v[pl.ds(t, 1), :] + local[pl.ds(t, 1), :] + row)

        act_each(pre, tails, put)
        return entering[points : points + 1]

    v0 = v_ref[...]
    before_copy.wait_recv()
    residual(v0, jnp.concatenate([before_in[...], v0[: points - 1]], axis=0), 0)
    ring_copies = correct(0)
    sum_local(0)

    for copy in whole_copies:
        copy.wait_recv()
    acc[0:nodes] = identity
    acc[nodes:] = identity

    def ring_step(k, _):
        j = ring - 1 - k
        m = lax.rem(z - j + ring, ring)
        sufrel[m] = acc[0:nodes]
        vmat[m] = acc[nodes:]
        new = product(acc[...], whole[m])
        acc[0:nodes] = new[0:nodes]
        acc[nodes:] = jnp.where(j < z, new[nodes:], acc[nodes:])
        return 0

    lax.fori_loop(0, ring, ring_step, 0)
    gwhole[0] = acc[0:nodes]
    gwhole_copies = [
        start(gwhole.at[0], gwhole.at[m], gwhole_sem.at[m], tm=group_peer(m)) for m in range(1, groups)
    ]
    group_copies = sum_ring(0, ring_copies)

    fz[0] = acc[nodes:]
    for m in range(1, groups):
        gwhole_copies[m - 1].wait_recv()
        fz[m] = product(fz[m - 1], gwhole[m])

    @pl.loop(0, ring // 2)
    def _(k):
        for i in range(2):
            m = 2 * k + i
            around = product(fz[groups - 1], sufrel[m])
            umat[m] = jnp.where((m >= 1) & (m <= z), vmat[m], around)

    def put_next(t, row):
        vnext[pl.ds(t, 1), :] = row

    def put_out(t, row):
        out_ref[pl.ds(t, 1), :] = row

    first = close(0, group_copies, v_ref, put_next)
    up_copies.append(start_next(vnext, up_in.at[1], up_sem.at[1]))

    v1 = vnext[...]
    residual(v1, jnp.concatenate([before_in[...] + first, v1[: points - 1]], axis=0), 1)
    ring_copies = correct(1)
    sum_local(1)
    group_copies = sum_ring(1, ring_copies)
    close(1, group_copies, vnext, put_out)

    for copy in started:
        copy.wait_send()

    @pl.when(part < parts - 1)
    def _():
        for copy in to_next + corr_copies:
            copy.wait_send()


def per_device(
    starting_voltage_guess,
    injected_amperes,
    capacitance,
    conductance,
    block_pattern,
    device_gain,
    link_weight,
    boundary_vertex_list,
    diagonal_reciprocals,
    boundary_jacobian,
    transfer,
    ring,
):
    points, _, nodes = starting_voltage_guess.shape
    count, parts = lax.axis_size("tm"), lax.axis_size("dom")
    groups = count // ring
    square = (nodes, nodes)
    vmem = pl.BlockSpec(memory_space=pltpu.VMEM)
    hbm = pl.BlockSpec(memory_space=pltpu.HBM)
    scratch = [
        pltpu.VMEM((points, nodes), F32),
        pltpu.VMEM((points, nodes), F32),
        pltpu.VMEM((1, nodes), F32),
        pltpu.VMEM(square, F32),
        pltpu.VMEM((1, 1, 1), jnp.int32),
        pltpu.VMEM((1, nodes), F32),
        pltpu.VMEM(square, F32),
        pltpu.VMEM((1, nodes), jnp.int32),
        pltpu.VMEM((points,) + square, F32),
        pltpu.VMEM(square, F32),
        pltpu.VMEM((points,) + square, F32),
        pltpu.VMEM((points // 2,) + square, F32),
        pltpu.VMEM((points // 4,) + square, F32),
        pltpu.VMEM((points // 8,) + square, F32),
        pltpu.VMEM((points,) + square, F32),
        pltpu.VMEM((points,) + square, F32),
        pltpu.VMEM((points,) + square, F32),
        pltpu.VMEM(square, F32),
        pltpu.VMEM((ring,) + square, F32),
        pltpu.VMEM((ring,) + square, F32),
        pltpu.VMEM((ring,) + square, F32),
        pltpu.VMEM((ring,) + square, F32),
        pltpu.VMEM((groups,) + square, F32),
        pltpu.VMEM((groups,) + square, F32),
        pltpu.VMEM((2 * nodes, nodes), F32),
        pltpu.VMEM((1, nodes), F32),
        pltpu.VMEM((1, nodes), jnp.int32),
        pltpu.VMEM((ITERS, points, nodes), F32),
        pltpu.VMEM((ITERS, points, nodes), F32),
        pltpu.VMEM((ITERS, points, nodes), F32),
        pltpu.VMEM((points, nodes), F32),
        pltpu.VMEM((points, nodes), F32),
        pltpu.VMEM((points, nodes), F32),
        pltpu.VMEM((ITERS, ring, 1, nodes), F32),
        pltpu.VMEM((ITERS, groups, 1, nodes), F32),
        pltpu.SemaphoreType.DMA((11,)),
        pltpu.SemaphoreType.DMA((3 + ITERS * 2 + 3 * (ring + groups),)),
        pltpu.SemaphoreType.DMA((ring,)),
        pltpu.SemaphoreType.DMA((groups,)),
        pltpu.SemaphoreType.DMA((ITERS, ring)),
        pltpu.SemaphoreType.DMA((ITERS, groups)),
        pltpu.SemaphoreType.DMA((2,)),
        pltpu.SemaphoreType.DMA((ITERS,)),
        pltpu.SemaphoreType.DMA((ITERS,)),
    ]
    out = pl.pallas_call(
        functools.partial(kernel, ring, groups, parts),
        out_shape=jax.ShapeDtypeStruct((points, nodes), F32),
        in_specs=[hbm] * 11,
        out_specs=vmem,
        scratch_shapes=scratch,
        compiler_params=pltpu.CompilerParams(
            collective_id=0, has_side_effects=True, vmem_limit_bytes=67_043_328
        ),
        name="newton",
    )(
        starting_voltage_guess[:, 0],
        injected_amperes[:, 0],
        capacitance,
        conductance[0],
        block_pattern,
        device_gain,
        link_weight[0],
        boundary_vertex_list,
        diagonal_reciprocals[:, 0, 0],
        boundary_jacobian[0],
        transfer[:, 0, 0],
    )
    return out[:, None]


def solution(mesh):
    in_specs = (
        P("tm", "dom", None),
        P("tm", "dom", None),
        P("dom", None),
        P("dom", None, None),
        P("dom", None, None),
        P("dom", None),
        P("dom", None, None),
        P("dom", None),
        P("tm", "dom", None, None, None),
        P("dom", None, None),
        P("tm", "dom", None, None, None),
    )
    out_specs = P("tm", "dom", None)
    count = mesh.shape["tm"]
    ring = 8 if count >= 64 else 2
    return jax.shard_map(
        functools.partial(per_device, ring=ring), mesh=mesh, in_specs=in_specs, out_specs=out_specs, check_vma=False
    )
```

```python
import functools

import jax
import jax.numpy as jnp
from jax import lax
from jax.experimental import pallas as pl
from jax.experimental.pallas import tpu as pltpu
from jax.sharding import PartitionSpec as P

ITERS = 2
F32 = jnp.float32
BF16 = jnp.bfloat16
NN = (((1,), (0,)), ((), ()))
NT = (((1,), (1,)), ((), ()))


def halves(x):
    high = x.astype(BF16)
    return high, (x - high.astype(F32)).astype(BF16)


def product(a, b, dims=NN):
    a_high, a_low = halves(a)
    b_high, b_low = halves(b)
    dot = functools.partial(lax.dot_general, dimension_numbers=dims, preferred_element_type=F32)
    return dot(a_high, b_high) + (dot(a_high, b_low) + dot(a_low, b_high))


def eye(n):
    return lax.broadcasted_iota(jnp.int32, (n, n), 0) == lax.broadcasted_iota(jnp.int32, (n, n), 1)


def as_row(square):
    column = jnp.sum(square, axis=1, keepdims=True)
    return jnp.sum(jnp.where(eye(square.shape[0]), column, 0.0), axis=0, keepdims=True)


def kernel(
    ring, groups, parts, v_hbm, inj_hbm, cap_hbm, cond_hbm, pat_hbm, gain_hbm, lw_hbm, bvl_hbm, dinv_hbm, bj_hbm, tr_hbm,
    out_ref, v_ref, inj_ref, cap_ref, cond_ref, pat_ref, gain_ref, lw_ref, bvl_ref, dinv_ref, bj_ref, tr_ref, pair2, pair4, pair8, pre, suf, coup, links_t, whole, sufrel, vmat, umat, gwhole, fz, acc,
    before_in, bvl_in, up_in, corr_in, corr, vnext, local, tails, bvec, bsum, share, far,
    load_sem, send_sem, whole_sem, gwhole_sem, bvec_sem, bsum_sem, small_sem, up_sem, corr_sem, far_send, far_sem,
):
    points, nodes = v_ref.shape
    tm, part = lax.axis_index("tm"), lax.axis_index("dom")
    count = ring * groups
    z, g = lax.rem(tm, ring), lax.div(tm, ring)

    def ring_peer(m):
        return g * ring + lax.rem(z + m, ring)

    def group_peer(m):
        return lax.rem(g + m, groups) * ring + z

    loads = {}
    for name, source, target in (
        ("tr", tr_hbm, tr_ref), ("v", v_hbm, v_ref), ("bvl", bvl_hbm, bvl_ref), ("lw", lw_hbm, lw_ref),
        ("bj", bj_hbm, bj_ref), ("dinv", dinv_hbm, dinv_ref), ("inj", inj_hbm, inj_ref), ("cap", cap_hbm, cap_ref),
        ("cond", cond_hbm, cond_ref), ("gain", gain_hbm, gain_ref), ("pat", pat_hbm, pat_ref),
    ):
        loads[name] = pltpu.make_async_copy(source, target, load_sem.at[len(loads)])
        loads[name].start()

    barrier = pltpu.get_barrier_semaphore()
    for m in range(1, ring):
        pl.semaphore_signal(barrier, inc=1, device_id={"tm": ring_peer(m)})
    for m in range(1, groups):
        pl.semaphore_signal(barrier, inc=1, device_id={"tm": group_peer(m)})
    for step in (1, count - 1):
        pl.semaphore_signal(barrier, inc=1, device_id={"tm": lax.rem(tm + step, count)})
    for step in (1, parts - 1):
        pl.semaphore_signal(barrier, inc=1, device_id={"dom": lax.rem(part + step, parts)})

    identity = jnp.where(eye(nodes), 1.0, 0.0)

    loads["tr"].wait()

    for source, target in ((tr_ref, pair2), (pair2, pair4), (pair4, pair8)):
        length = target.shape[0]
        inner = min(4, length)

        @pl.loop(0, length // inner)
        def _(k):
            for i in range(inner):
                e = k * inner + i
                target[e] = product(source[2 * e + 1], source[2 * e])

    whole[0] = product(pair8[1], pair8[0])

    for name in loads:
        if name != "tr":
            loads[name].wait()
    pl.semaphore_wait(barrier, ring - 1 + groups - 1 + 4)

    started = []

    def send(source, target, index, sem, **where):
        copy = pltpu.make_async_remote_copy(
            src_ref=source, dst_ref=target, send_sem=send_sem.at[index], recv_sem=sem,
            device_id=where, device_id_type=pl.DeviceIdType.MESH,
        )
        return copy

    index = iter(range(1000))

    def start(source, target, sem, **where):
        copy = send(source, target, next(index), sem, **where)
        copy.start()
        started.append(copy)
        return copy

    to_next = []

    def start_next(source, target, sem):
        copy = send(source, target, next(index), sem, dom=lax.rem(part + 1, parts))

        @pl.when(part < parts - 1)
        def _():
            copy.start()

        to_next.append(copy)
        return copy

    before_copy = start(v_ref.at[points - 1 :], before_in, small_sem.at[0], tm=lax.rem(tm + 1, count))
    bvl_copy = start_next(bvl_ref, bvl_in, small_sem.at[1])
    up_copies = [start_next(v_ref, up_in.at[0], up_sem.at[0])]
    half = nodes // 2
    top, bottom = pl.ds(0, half), pl.ds(half, half)

    def pass_on(slot, rows, hop, target):
        side = 0 if rows is top else 1
        return start(
            whole.at[slot, rows], whole.at[target, rows], whole_sem.at[target, side], tm=ring_peer(hop)
        )

    whole_copies = {}
    if ring == 8:
        for rows, hop in ((top, 2), (bottom, 6), (bottom, 2), (top, 6), (top, 1), (bottom, 7), (bottom, 1), (top, 7)):
            whole_copies[hop, rows is top] = pass_on(0, rows, hop, hop)
    else:
        for hop in range(1, ring):
            for rows in (top, bottom):
                whole_copies[hop, rows is top] = pass_on(0, rows, hop, hop)

    def forward_ring():
        if ring != 8:
            return
        for slot, rows, last in ((2, top, True), (6, bottom, True), (2, bottom, False), (6, top, False)):
            whole_copies.pop((slot, rows is top)).wait_recv()
            if last:
                whole_copies[4, rows is top] = pass_on(slot, rows, slot, 4)
            side = 1 if slot == 2 else 7
            target = 3 if slot == 2 else 5
            whole_copies[target, rows is top] = pass_on(slot, rows, side, target)

    pre[0] = tr_ref[0]
    pre[1] = pair2[0]
    pre[3] = pair4[0]
    pre[7] = pair8[0]
    pre[15] = whole[0]
    pre[5] = product(pair2[2], pair4[0])
    pre[9] = product(pair2[4], pair8[0])
    pre[11] = product(pair4[2], pair8[0])
    pre[13] = product(pair2[6], pre[11])
    suf[15] = identity
    suf[14] = tr_ref[15]
    suf[13] = pair2[7]
    suf[11] = pair4[3]
    suf[7] = pair8[1]
    suf[9] = product(pair4[3], pair2[5])
    suf[5] = product(pair8[1], pair2[3])
    suf[3] = product(pair8[1], pair4[1])
    suf[1] = product(suf[3], pair2[1])

    @pl.loop(0, 7)
    def _(k):
        pre[2 * k + 2] = product(tr_ref[2 * k + 2], pre[2 * k + 1])
        suf[2 * k] = product(suf[2 * k + 1], tr_ref[2 * k + 1])

    forward_ring()

    @pl.when(part > 0)
    def _():
        bvl_copy.wait_recv()
        row = lax.broadcasted_iota(jnp.int32, (nodes, nodes), 0)
        spread = jnp.where(row == bvl_in[...], 1.0, 0.0)
        links_t[...] = product(spread, lw_ref[...], NT)
        acc[0:nodes] = product(bj_ref[...], spread, NT)

        @pl.loop(0, points // 2)
        def _(k):
            for i in range(2):
                coup[2 * k + i] = product(dinv_ref[2 * k + i], acc[0:nodes])

    effective = cond_ref[...] * pat_ref[0].astype(F32)

    def residual(v, before, it):
        r = (
            inj_ref[...]
            - cap_ref[...] * (v - before)
            - product(v, effective, NT)
            - gain_ref[...] * jnp.tanh(v)
        )
        local[...] = r

        @pl.when(part > 0)
        def _():
            up_copies[it].wait_recv()
            local[...] = local[...] + product(up_in[it], links_t[...])

    def act_each(matrices, vectors, store):
        @pl.loop(0, points // 4)
        def _(k):
            for i in range(4):
                t = 4 * k + i
                store(t, as_row(matrices[t] * vectors[pl.ds(t, 1), :]))

    corr_copies = []

    def correct(it):
        def put(t, row):
            corr[it, pl.ds(t, 1), :] = row

        def add(t, row):
            corr[it, pl.ds(t, 1), :] = corr[it, pl.ds(t, 1), :] + row

        act_each(dinv_ref, local, put)
        corr_copies.append(
            send(corr.at[it], corr_in.at[it], next(index), corr_sem.at[it], dom=lax.rem(part + 1, parts))
        )

        @pl.when(part > 0)
        def _():
            corr_copies[it].wait_recv()
            act_each(coup, corr_in.at[it], add)

        @pl.when(part < parts - 1)
        def _():
            corr_copies[it].start()

        total = suf[0] * corr[it, 0:1, :]
        for t in range(1, points):
            total = total + suf[t] * corr[it, t : t + 1, :]
        bvec[it, 0] = as_row(total)
        return [
            start(bvec.at[it, 0], bvec.at[it, m], bvec_sem.at[it, m], tm=ring_peer(m)) for m in range(1, ring)
        ]

    def sum_local(it):
        def step(t, x):
            x = as_row(tr_ref[t] * x) + corr[it, pl.ds(t, 1), :]
            local[pl.ds(t, 1), :] = x
            return x

        lax.fori_loop(0, points, step, jnp.zeros((1, nodes), F32))

        def put(t, row):
            tails[pl.ds(t, 1), :] = row

        act_each(suf, corr.at[it], put)
        running = jnp.zeros((1, nodes), F32)
        for t in range(points - 1, -1, -1):
            own = tails[t : t + 1, :]
            tails[t : t + 1, :] = running
            running = running + own

    def sum_ring(copies):
        total = sufrel[0] * bvec[0, 0]
        for m in range(1, ring):
            copies[m - 1].wait_recv()
            total = total + sufrel[m] * bvec[0, m]
        bsum[0] = as_row(total)
        return [start(bsum.at[0], bsum.at[m], bsum_sem.at[m], tm=group_peer(m)) for m in range(1, groups)]

    def send_far():
        share[...] = as_row(sufrel[0] * bvec[1, 0])
        for m in range(groups - 1, 0, -1):
            for r in range(ring):
                pltpu.make_async_remote_copy(
                    src_ref=share, dst_ref=far.at[m, pl.ds(r, 1)], send_sem=far_send, recv_sem=far_sem,
                    device_id={"tm": lax.rem(g + m, groups) * ring + lax.rem(z + r, ring)},
                    device_id_type=pl.DeviceIdType.MESH,
                ).start()

    all_far = pltpu.make_async_remote_copy(
        src_ref=far.at[pl.ds(1, groups - 1)], dst_ref=far.at[pl.ds(1, groups - 1)], send_sem=far_send,
        recv_sem=far_sem, device_id={"tm": ring_peer(1)}, device_id_type=pl.DeviceIdType.MESH,
    )

    def close(it, group_sums, v, store):
        for copy in ring_copies[it]:
            if it > 0:
                copy.wait_recv()
        near = umat[1] * bvec[it, 1]
        for m in range(2, ring):
            near = near + umat[m] * bvec[it, m]
        wrapped = product(jnp.concatenate([tails[...], jnp.broadcast_to(bvec[it, 0], (8, nodes))], axis=0), umat[0], NT)
        for m, arrived in enumerate(group_sums(), 1):
            near = near + fz[m - 1] * arrived
        entering = wrapped + as_row(near)
        tails[...] = entering[0:points]

        def put(t, row):
            store(t, v[pl.ds(t, 1), :] + local[pl.ds(t, 1), :] + row)

        act_each(pre, tails, put)
        return entering[points : points + 1]

    v0 = v_ref[...]
    before_copy.wait_recv()
    residual(v0, jnp.concatenate([before_in[...], v0[: points - 1]], axis=0), 0)
    ring_copies = [correct(0)]
    sum_local(0)

    for copy in list(whole_copies.values()):
        copy.wait_recv()
    acc[0:nodes] = identity
    acc[nodes:] = identity

    def ring_step(k, _):
        j = ring - 1 - k
        m = lax.rem(z - j + ring, ring)
        sufrel[m] = acc[0:nodes]
        vmat[m] = acc[nodes:]
        new = product(acc[...], whole[m])
        acc[0:nodes] = new[0:nodes]
        acc[nodes:] = jnp.where(j < z, new[nodes:], acc[nodes:])
        return 0

    lax.fori_loop(0, ring, ring_step, 0)
    gwhole[0] = acc[0:nodes]
    gwhole_copies = [
        start(gwhole.at[0], gwhole.at[m], gwhole_sem.at[m], tm=group_peer(m)) for m in range(1, groups)
    ]
    group_copies = sum_ring(ring_copies[0])

    fz[0] = acc[nodes:]
    for m in range(1, groups):
        gwhole_copies[m - 1].wait_recv()
        fz[m] = product(fz[m - 1], gwhole[m])

    @pl.loop(0, ring // 2)
    def _(k):
        for i in range(2):
            m = 2 * k + i
            around = product(fz[groups - 1], sufrel[m])
            umat[m] = jnp.where((m >= 1) & (m <= z), vmat[m], around)

    def put_next(t, row):
        vnext[pl.ds(t, 1), :] = row

    def put_out(t, row):
        out_ref[pl.ds(t, 1), :] = row

    def near_sums():
        for m in range(1, groups):
            group_copies[m - 1].wait_recv()
            yield bsum[m]

    def far_sums():
        all_far.wait_recv()
        for m in range(1, groups):
            yield jnp.sum(far[m], axis=0, keepdims=True)

    first = close(0, near_sums, v_ref, put_next)
    up_copies.append(start_next(vnext, up_in.at[1], up_sem.at[1]))

    v1 = vnext[...]
    residual(v1, jnp.concatenate([before_in[...] + first, v1[: points - 1]], axis=0), 1)
    ring_copies.append(correct(1))
    send_far()
    sum_local(1)
    close(1, far_sums, vnext, put_out)
    all_far.wait_send()

    for copy in started:
        copy.wait_send()

    @pl.when(part < parts - 1)
    def _():
        for copy in to_next + corr_copies:
            copy.wait_send()


def per_device(
    starting_voltage_guess,
    injected_amperes,
    capacitance,
    conductance,
    block_pattern,
    device_gain,
    link_weight,
    boundary_vertex_list,
    diagonal_reciprocals,
    boundary_jacobian,
    transfer,
    ring,
):
    points, _, nodes = starting_voltage_guess.shape
    count, parts = lax.axis_size("tm"), lax.axis_size("dom")
    groups = count // ring
    square = (nodes, nodes)
    vmem = pl.BlockSpec(memory_space=pltpu.VMEM)
    hbm = pl.BlockSpec(memory_space=pltpu.HBM)
    scratch = [
        pltpu.VMEM((points, nodes), F32),
        pltpu.VMEM((points, nodes), F32),
        pltpu.VMEM((1, nodes), F32),
        pltpu.VMEM(square, F32),
        pltpu.VMEM((1, 1, 1), jnp.int32),
        pltpu.VMEM((1, nodes), F32),
        pltpu.VMEM(square, F32),
        pltpu.VMEM((1, nodes), jnp.int32),
        pltpu.VMEM((points,) + square, F32),
        pltpu.VMEM(square, F32),
        pltpu.VMEM((points,) + square, F32),
        pltpu.VMEM((points // 2,) + square, F32),
        pltpu.VMEM((points // 4,) + square, F32),
        pltpu.VMEM((points // 8,) + square, F32),
        pltpu.VMEM((points,) + square, F32),
        pltpu.VMEM((points,) + square, F32),
        pltpu.VMEM((points,) + square, F32),
        pltpu.VMEM(square, F32),
        pltpu.VMEM((ring,) + square, F32),
        pltpu.VMEM((ring,) + square, F32),
        pltpu.VMEM((ring,) + square, F32),
        pltpu.VMEM((ring,) + square, F32),
        pltpu.VMEM((groups,) + square, F32),
        pltpu.VMEM((groups,) + square, F32),
        pltpu.VMEM((2 * nodes, nodes), F32),
        pltpu.VMEM((1, nodes), F32),
        pltpu.VMEM((1, nodes), jnp.int32),
        pltpu.VMEM((ITERS, points, nodes), F32),
        pltpu.VMEM((ITERS, points, nodes), F32),
        pltpu.VMEM((ITERS, points, nodes), F32),
        pltpu.VMEM((points, nodes), F32),
        pltpu.VMEM((points, nodes), F32),
        pltpu.VMEM((points, nodes), F32),
        pltpu.VMEM((ITERS, ring, 1, nodes), F32),
        pltpu.VMEM((groups, 1, nodes), F32),
        pltpu.VMEM((1, nodes), F32),
        pltpu.VMEM((groups, ring, nodes), F32),
        pltpu.SemaphoreType.DMA((11,)),
        pltpu.SemaphoreType.DMA((3 + ITERS * 2 + 4 * (ring + groups),)),
        pltpu.SemaphoreType.DMA((ring, 2)),
        pltpu.SemaphoreType.DMA((groups,)),
        pltpu.SemaphoreType.DMA((ITERS, ring)),
        pltpu.SemaphoreType.DMA((groups,)),
        pltpu.SemaphoreType.DMA((2,)),
        pltpu.SemaphoreType.DMA((ITERS,)),
        pltpu.SemaphoreType.DMA((ITERS,)),
        pltpu.SemaphoreType.DMA,
        pltpu.SemaphoreType.DMA,
    ]
    out = pl.pallas_call(
        functools.partial(kernel, ring, groups, parts),
        out_shape=pltpu.VMEM((points, nodes), F32),
        in_specs=[hbm] * 11,
        out_specs=vmem,
        scratch_shapes=scratch,
        compiler_params=pltpu.CompilerParams(
            collective_id=0, has_side_effects=True, vmem_limit_bytes=66_000_000
        ),
        name="newton",
    )(
        starting_voltage_guess[:, 0],
        injected_amperes[:, 0],
        capacitance,
        conductance[0],
        block_pattern,
        device_gain,
        link_weight[0],
        boundary_vertex_list,
        diagonal_reciprocals[:, 0, 0],
        boundary_jacobian[0],
        transfer[:, 0, 0],
    )
    return out[:, None]


def solution(mesh):
    in_specs = (
        P("tm", "dom", None),
        P("tm", "dom", None),
        P("dom", None),
        P("dom", None, None),
        P("dom", None, None),
        P("dom", None),
        P("dom", None, None),
        P("dom", None),
        P("tm", "dom", None, None, None),
        P("dom", None, None),
        P("tm", "dom", None, None, None),
    )
    out_specs = P("tm", "dom", None)
    count = mesh.shape["tm"]
    ring = 8 if count >= 64 else 2
    return jax.shard_map(
        functools.partial(per_device, ring=ring), mesh=mesh, in_specs=in_specs, out_specs=out_specs, check_vma=False
    )
```

```python
import functools

import jax
import jax.numpy as jnp
from jax import lax
from jax.experimental import pallas as pl
from jax.experimental.pallas import tpu as pltpu
from jax.sharding import PartitionSpec as P

ITERS = 2
F32 = jnp.float32
BF16 = jnp.bfloat16
NN = (((1,), (0,)), ((), ()))
NT = (((1,), (1,)), ((), ()))


def halves(x):
    high = x.astype(BF16)
    return high, (x - high.astype(F32)).astype(BF16)


def product(a, b, dims=NN):
    a_high, a_low = halves(a)
    b_high, b_low = halves(b)
    dot = functools.partial(lax.dot_general, dimension_numbers=dims, preferred_element_type=F32)
    return dot(a_high, b_high) + (dot(a_high, b_low) + dot(a_low, b_high))


def eye(n):
    return lax.broadcasted_iota(jnp.int32, (n, n), 0) == lax.broadcasted_iota(jnp.int32, (n, n), 1)


def as_row(square):
    column = jnp.sum(square, axis=1, keepdims=True)
    return jnp.sum(jnp.where(eye(square.shape[0]), column, 0.0), axis=0, keepdims=True)


def kernel(
    ring, groups, parts, v_hbm, inj_hbm, cap_hbm, cond_hbm, pat_hbm, gain_hbm, lw_hbm, bvl_hbm, dinv_hbm, bj_hbm, tr_hbm,
    out_ref, v_ref, inj_ref, cap_ref, cond_ref, pat_ref, gain_ref, lw_ref, bvl_ref, dinv_ref, bj_ref, tr_ref, pair2, pair4, pair8, pre, suf, coup, links_t, whole, sufrel, vmat, gwhole, fz, acc,
    before_in, bvl_in, up_in, corr_in, corr, vnext, local, tails, bvec, bsum, share, far, near_sum, far_side, coup2, lead, lead_in,
    load_sem, send_sem, whole_sem, gwhole_sem, bvec_sem, bsum_sem, small_sem, up_sem, corr_sem, far_send, far_sem,
):
    points, nodes = v_ref.shape
    tm, part = lax.axis_index("tm"), lax.axis_index("dom")
    count = ring * groups
    z, g = lax.rem(tm, ring), lax.div(tm, ring)

    def ring_peer(m):
        return g * ring + lax.rem(z + m, ring)

    def group_peer(m):
        return lax.rem(g + m, groups) * ring + z

    loads = {}
    for name, source, target in (
        ("tr", tr_hbm, tr_ref), ("v", v_hbm, v_ref), ("bvl", bvl_hbm, bvl_ref), ("lw", lw_hbm, lw_ref),
        ("bj", bj_hbm, bj_ref), ("dinv", dinv_hbm, dinv_ref), ("inj", inj_hbm, inj_ref), ("cap", cap_hbm, cap_ref),
        ("cond", cond_hbm, cond_ref), ("gain", gain_hbm, gain_ref), ("pat", pat_hbm, pat_ref),
    ):
        loads[name] = pltpu.make_async_copy(source, target, load_sem.at[len(loads)])
        loads[name].start()

    barrier = pltpu.get_barrier_semaphore()
    for m in range(1, ring):
        pl.semaphore_signal(barrier, inc=1, device_id={"tm": ring_peer(m)})
    for m in range(1, groups):
        pl.semaphore_signal(barrier, inc=1, device_id={"tm": group_peer(m)})
    for step in (1, count - 1):
        pl.semaphore_signal(barrier, inc=1, device_id={"tm": lax.rem(tm + step, count)})
    for step in (1, parts - 1):
        pl.semaphore_signal(barrier, inc=1, device_id={"dom": lax.rem(part + step, parts)})

    identity = jnp.where(eye(nodes), 1.0, 0.0)

    loads["tr"].wait()

    for source, target in ((tr_ref, pair2), (pair2, pair4), (pair4, pair8)):
        length = target.shape[0]
        inner = min(4, length)

        @pl.loop(0, length // inner)
        def _(k):
            for i in range(inner):
                e = k * inner + i
                target[e] = product(source[2 * e + 1], source[2 * e])

    whole[0] = product(pair8[1], pair8[0])

    for name in loads:
        if name != "tr":
            loads[name].wait()
    pl.semaphore_wait(barrier, ring - 1 + groups - 1 + 4)

    started = []

    def send(source, target, index, sem, **where):
        copy = pltpu.make_async_remote_copy(
            src_ref=source, dst_ref=target, send_sem=send_sem.at[index], recv_sem=sem,
            device_id=where, device_id_type=pl.DeviceIdType.MESH,
        )
        return copy

    index = iter(range(1000))

    def start(source, target, sem, **where):
        copy = send(source, target, next(index), sem, **where)
        copy.start()
        started.append(copy)
        return copy

    to_next = []

    def start_next(source, target, sem):
        copy = send(source, target, next(index), sem, dom=lax.rem(part + 1, parts))

        @pl.when(part < parts - 1)
        def _():
            copy.start()

        to_next.append(copy)
        return copy

    before_copy = start(v_ref.at[points - 1 :], before_in, small_sem.at[0], tm=lax.rem(tm + 1, count))
    bvl_copy = start_next(bvl_ref, bvl_in, small_sem.at[1])
    up_copies = [start_next(v_ref, up_in.at[0], up_sem.at[0])]
    half = nodes // 2
    top, bottom = pl.ds(0, half), pl.ds(half, half)

    def pass_on(slot, rows, hop, target):
        side = 0 if rows is top else 1
        return start(
            whole.at[slot, rows], whole.at[target, rows], whole_sem.at[target, side], tm=ring_peer(hop)
        )

    whole_copies = {}
    if ring == 8:
        for rows, hop in ((top, 2), (bottom, 6), (bottom, 2), (top, 6), (top, 1), (bottom, 7), (bottom, 1), (top, 7)):
            whole_copies[hop, rows is top] = pass_on(0, rows, hop, hop)
    else:
        for hop in range(1, ring):
            for rows in (top, bottom):
                whole_copies[hop, rows is top] = pass_on(0, rows, hop, hop)

    def forward_ring():
        if ring != 8:
            return
        for slot, rows, last in ((2, top, True), (6, bottom, True), (2, bottom, False), (6, top, False)):
            whole_copies.pop((slot, rows is top)).wait_recv()
            if last:
                whole_copies[4, rows is top] = pass_on(slot, rows, slot, 4)
            side = 1 if slot == 2 else 7
            target = 3 if slot == 2 else 5
            whole_copies[target, rows is top] = pass_on(slot, rows, side, target)

    suf[15] = identity
    suf[14] = tr_ref[15]
    suf[13] = pair2[7]
    suf[11] = pair4[3]
    suf[7] = pair8[1]
    suf[9] = product(pair4[3], pair2[5])
    suf[5] = product(pair8[1], pair2[3])
    suf[3] = product(pair8[1], pair4[1])
    suf[1] = product(suf[3], pair2[1])
    for k in range(7):
        suf[2 * k] = product(suf[2 * k + 1], tr_ref[2 * k + 1])

    @pl.when(part > 0)
    def _():
        bvl_copy.wait_recv()
        row = lax.broadcasted_iota(jnp.int32, (nodes, nodes), 0)
        spread = jnp.where(row == bvl_in[...], 1.0, 0.0)
        links_t[...] = product(spread, lw_ref[...], NT)
        acc[0:nodes] = product(bj_ref[...], spread, NT)

        @pl.loop(0, points // 2)
        def _(k):
            for i in range(2):
                coup[2 * k + i] = product(dinv_ref[2 * k + i], acc[0:nodes])

    effective = cond_ref[...] * pat_ref[0].astype(F32)

    def residual(v, before, it):
        r = (
            inj_ref[...]
            - cap_ref[...] * (v - before)
            - product(v, effective, NT)
            - gain_ref[...] * jnp.tanh(v)
        )
        local[...] = r

        @pl.when(part > 0)
        def _():
            up_copies[it].wait_recv()
            local[...] = local[...] + product(up_in[it], links_t[...])

    def act_each(matrices, vectors, store):
        for t in range(points):
            store(t, as_row(matrices[t] * vectors[t : t + 1, :]))

    corr_copies = []
    lead_copy = send(lead, lead_in, next(index), small_sem.at[2], dom=lax.rem(part + 1, parts))
    coup_copy = send(coup, coup2, next(index), small_sem.at[3], dom=lax.rem(part + 1, parts))
    second_copy = send(corr.at[1], corr_in.at[1], next(index), corr_sem.at[1], dom=lax.rem(part + 2, parts))

    @pl.when(part == 2)
    def _():
        coup_copy.start()

    def skip_ahead():
        @pl.when(part == 3)
        def _():
            coup_copy.wait_recv()
            for t in range(points):
                coup2[t] = product(coup[t], coup2[t])

    def correct(it):
        def put(t, row):
            corr[it, pl.ds(t, 1), :] = row

        def add(t, row):
            corr[it, pl.ds(t, 1), :] = corr[it, pl.ds(t, 1), :] + row

        act_each(dinv_ref, local, put)
        if it == 0:
            forward_ring()
        corr_copies.append(
            send(corr.at[it], corr_in.at[it], next(index), corr_sem.at[it], dom=lax.rem(part + 1, parts))
        )

        if it == 0 or parts != 4:

            @pl.when(part > 0)
            def _():
                corr_copies[it].wait_recv()
                act_each(coup, corr_in.at[it], add)

            @pl.when(part < parts - 1)
            def _():
                corr_copies[it].start()
        else:

            @pl.when(part == 2)
            def _():
                lead[...] = corr[it]
                lead_copy.start()

            @pl.when((part == 1) | (part == 2))
            def _():
                corr_copies[it].wait_recv()
                act_each(coup, corr_in.at[it], add)

            @pl.when(part == 3)
            def _():
                lead_copy.wait_recv()
                act_each(coup, lead_in, add)
                corr_copies[it].wait_recv()
                act_each(coup2, corr_in.at[it], add)

            @pl.when(part < 2)
            def _():
                corr_copies[it].start()

            @pl.when(part == 1)
            def _():
                second_copy.start()

        total = suf[0] * corr[it, 0:1, :]
        for t in range(1, points):
            total = total + suf[t] * corr[it, t : t + 1, :]
        bvec[it, 0] = as_row(total)
        return [
            start(bvec.at[it, 0], bvec.at[it, m], bvec_sem.at[it, m], tm=ring_peer(m)) for m in range(1, ring)
        ]

    def sum_local(it):
        def step(t, x):
            x = as_row(tr_ref[t] * x) + corr[it, pl.ds(t, 1), :]
            local[pl.ds(t, 1), :] = x
            return x

        lax.fori_loop(0, points, step, jnp.zeros((1, nodes), F32))

        def put(t, row):
            tails[pl.ds(t, 1), :] = row

        act_each(suf, corr.at[it], put)
        running = jnp.zeros((1, nodes), F32)
        for t in range(points - 1, -1, -1):
            own = tails[t : t + 1, :]
            tails[t : t + 1, :] = running
            running = running + own

    def sum_ring(copies):
        total = sufrel[0] * bvec[0, 0]
        for m in range(1, ring):
            copies[m - 1].wait_recv()
            total = total + sufrel[m] * bvec[0, m]
        bsum[0] = as_row(total)
        return [start(bsum.at[0], bsum.at[m], bsum_sem.at[m], tm=group_peer(m)) for m in range(1, groups)]

    def send_far():
        share[...] = as_row(sufrel[0] * bvec[1, 0])
        for m in range(groups - 1, 0, -1):
            for r in range(ring):
                pltpu.make_async_remote_copy(
                    src_ref=share, dst_ref=far.at[m, pl.ds(r, 1)], send_sem=far_send, recv_sem=far_sem,
                    device_id={"tm": lax.rem(g + m, groups) * ring + lax.rem(z + r, ring)},
                    device_id_type=pl.DeviceIdType.MESH,
                ).start()

    all_far = pltpu.make_async_remote_copy(
        src_ref=far.at[pl.ds(1, groups - 1)], dst_ref=far.at[pl.ds(1, groups - 1)], send_sem=far_send,
        recv_sem=far_sem, device_id={"tm": ring_peer(1)}, device_id_type=pl.DeviceIdType.MESH,
    )

    def gather_near(it):
        if it > 0:
            for copy in ring_copies[it]:
                copy.wait_recv()
        near = jnp.zeros((nodes, nodes), F32)
        after = jnp.zeros((nodes, nodes), F32)
        for m in range(1, ring):
            behind = m <= z
            term = jnp.where(behind, vmat[m], sufrel[m]) * bvec[it, m]
            near = near + jnp.where(behind, term, 0.0)
            after = after + jnp.where(behind, 0.0, term)
        near_sum[...] = as_row(near)
        own = jnp.concatenate([tails[...], jnp.broadcast_to(bvec[it, 0], (8, nodes))], axis=0)
        far_side[...] = product(own, sufrel[0], NT) + as_row(after)

    def close(it, group_sums, v, store):
        wrapped = product(far_side[...], fz[groups - 1], NT) + near_sum[...]
        near = jnp.zeros((nodes, nodes), F32)
        for m, arrived in enumerate(group_sums(), 1):
            near = near + fz[m - 1] * arrived
        entering = wrapped + as_row(near)
        tails[...] = entering[0:points]

        def put(t, row):
            store(t, v[pl.ds(t, 1), :] + local[pl.ds(t, 1), :] + row)

        act_each(pre, tails, put)
        return entering[points : points + 1]

    v0 = v_ref[...]
    before_copy.wait_recv()
    residual(v0, jnp.concatenate([before_in[...], v0[: points - 1]], axis=0), 0)
    ring_copies = [correct(0)]
    for copy in list(whole_copies.values()):
        copy.wait_recv()

    def ring_slot(j):
        return lax.rem(z - j + ring, ring)

    trees = [whole[ring_slot(j)] for j in range(ring)]
    while len(trees) > 1:
        trees = [product(trees[k + 1], trees[k]) for k in range(0, len(trees), 2)]
    gwhole[0] = trees[0]
    gwhole_copies = [
        start(gwhole.at[0], gwhole.at[m], gwhole_sem.at[m], tm=group_peer(m)) for m in range(1, groups)
    ]
    acc[0:nodes] = identity
    acc[nodes:] = identity

    def ring_step(k, _):
        j = ring - 1 - k
        m = ring_slot(j)
        sufrel[m] = acc[0:nodes]
        vmat[m] = acc[nodes:]
        new = product(acc[...], whole[m])
        acc[0:nodes] = new[0:nodes]
        acc[nodes:] = jnp.where(j < z, new[nodes:], acc[nodes:])
        return 0

    lax.fori_loop(0, ring, ring_step, 0)
    group_copies = sum_ring(ring_copies[0])

    sum_local(0)
    gather_near(0)

    pre[0] = tr_ref[0]
    pre[1] = pair2[0]
    pre[3] = pair4[0]
    pre[7] = pair8[0]
    pre[15] = whole[0]
    pre[5] = product(pair2[2], pair4[0])
    pre[9] = product(pair2[4], pair8[0])
    pre[11] = product(pair4[2], pair8[0])
    pre[13] = product(pair2[6], pre[11])
    for k in range(7):
        pre[2 * k + 2] = product(tr_ref[2 * k + 2], pre[2 * k + 1])

    skip_ahead()

    fz[0] = acc[nodes:]
    for m in range(1, groups):
        gwhole_copies[m - 1].wait_recv()
        fz[m] = product(fz[m - 1], gwhole[m])

    def put_next(t, row):
        vnext[pl.ds(t, 1), :] = row

    def put_out(t, row):
        out_ref[pl.ds(t, 1), :] = row

    def near_sums():
        for m in range(1, groups):
            group_copies[m - 1].wait_recv()
            yield bsum[m]

    def far_sums():
        all_far.wait_recv()
        for m in range(1, groups):
            yield jnp.sum(far[m], axis=0, keepdims=True)

    first = close(0, near_sums, v_ref, put_next)
    up_copies.append(start_next(vnext, up_in.at[1], up_sem.at[1]))

    v1 = vnext[...]
    residual(v1, jnp.concatenate([before_in[...] + first, v1[: points - 1]], axis=0), 1)
    ring_copies.append(correct(1))
    send_far()
    sum_local(1)
    gather_near(1)
    close(1, far_sums, vnext, put_out)
    all_far.wait_send()

    for copy in started:
        copy.wait_send()

    @pl.when(part < parts - 1)
    def _():
        for copy in to_next + corr_copies[:1]:
            copy.wait_send()

    @pl.when(part < (2 if parts == 4 else parts - 1))
    def _():
        corr_copies[1].wait_send()

    @pl.when(part == 1)
    def _():
        if parts == 4:
            second_copy.wait_send()

    @pl.when(part == 2)
    def _():
        lead_copy.wait_send()
        coup_copy.wait_send()


def per_device(
    starting_voltage_guess,
    injected_amperes,
    capacitance,
    conductance,
    block_pattern,
    device_gain,
    link_weight,
    boundary_vertex_list,
    diagonal_reciprocals,
    boundary_jacobian,
    transfer,
    ring,
):
    points, _, nodes = starting_voltage_guess.shape
    count, parts = lax.axis_size("tm"), lax.axis_size("dom")
    groups = count // ring
    square = (nodes, nodes)
    vmem = pl.BlockSpec(memory_space=pltpu.VMEM)
    hbm = pl.BlockSpec(memory_space=pltpu.HBM)
    scratch = [
        pltpu.VMEM((points, nodes), F32),
        pltpu.VMEM((points, nodes), F32),
        pltpu.VMEM((1, nodes), F32),
        pltpu.VMEM(square, F32),
        pltpu.VMEM((1, 1, 1), jnp.int32),
        pltpu.VMEM((1, nodes), F32),
        pltpu.VMEM(square, F32),
        pltpu.VMEM((1, nodes), jnp.int32),
        pltpu.VMEM((points,) + square, F32),
        pltpu.VMEM(square, F32),
        pltpu.VMEM((points,) + square, F32),
        pltpu.VMEM((points // 2,) + square, F32),
        pltpu.VMEM((points // 4,) + square, F32),
        pltpu.VMEM((points // 8,) + square, F32),
        pltpu.VMEM((points,) + square, F32),
        pltpu.VMEM((points,) + square, F32),
        pltpu.VMEM((points,) + square, F32),
        pltpu.VMEM(square, F32),
        pltpu.VMEM((ring,) + square, F32),
        pltpu.VMEM((ring,) + square, F32),
        pltpu.VMEM((ring,) + square, F32),
        pltpu.VMEM((groups,) + square, F32),
        pltpu.VMEM((groups,) + square, F32),
        pltpu.VMEM((2 * nodes, nodes), F32),
        pltpu.VMEM((1, nodes), F32),
        pltpu.VMEM((1, nodes), jnp.int32),
        pltpu.VMEM((ITERS, points, nodes), F32),
        pltpu.VMEM((ITERS, points, nodes), F32),
        pltpu.VMEM((ITERS, points, nodes), F32),
        pltpu.VMEM((points, nodes), F32),
        pltpu.VMEM((points, nodes), F32),
        pltpu.VMEM((points, nodes), F32),
        pltpu.VMEM((ITERS, ring, 1, nodes), F32),
        pltpu.VMEM((groups, 1, nodes), F32),
        pltpu.VMEM((1, nodes), F32),
        pltpu.VMEM((groups, ring, nodes), F32),
        pltpu.VMEM((1, nodes), F32),
        pltpu.VMEM((points + 8, nodes), F32),
        pltpu.VMEM((points,) + square, F32),
        pltpu.VMEM((points, nodes), F32),
        pltpu.VMEM((points, nodes), F32),
        pltpu.SemaphoreType.DMA((11,)),
        pltpu.SemaphoreType.DMA((6 + ITERS * 2 + 4 * (ring + groups),)),
        pltpu.SemaphoreType.DMA((ring, 2)),
        pltpu.SemaphoreType.DMA((groups,)),
        pltpu.SemaphoreType.DMA((ITERS, ring)),
        pltpu.SemaphoreType.DMA((groups,)),
        pltpu.SemaphoreType.DMA((4,)),
        pltpu.SemaphoreType.DMA((ITERS,)),
        pltpu.SemaphoreType.DMA((ITERS,)),
        pltpu.SemaphoreType.DMA,
        pltpu.SemaphoreType.DMA,
    ]
    out = pl.pallas_call(
        functools.partial(kernel, ring, groups, parts),
        out_shape=pltpu.VMEM((points, nodes), F32),
        in_specs=[hbm] * 11,
        out_specs=vmem,
        scratch_shapes=scratch,
        compiler_params=pltpu.CompilerParams(
            collective_id=0, has_side_effects=True, vmem_limit_bytes=66_000_000
        ),
        name="newton",
    )(
        starting_voltage_guess[:, 0],
        injected_amperes[:, 0],
        capacitance,
        conductance[0],
        block_pattern,
        device_gain,
        link_weight[0],
        boundary_vertex_list,
        diagonal_reciprocals[:, 0, 0],
        boundary_jacobian[0],
        transfer[:, 0, 0],
    )
    return out[:, None]


def solution(mesh):
    in_specs = (
        P("tm", "dom", None),
        P("tm", "dom", None),
        P("dom", None),
        P("dom", None, None),
        P("dom", None, None),
        P("dom", None),
        P("dom", None, None),
        P("dom", None),
        P("tm", "dom", None, None, None),
        P("dom", None, None),
        P("tm", "dom", None, None, None),
    )
    out_specs = P("tm", "dom", None)
    count = mesh.shape["tm"]
    ring = 8 if count >= 64 else 2
    return jax.shard_map(
        functools.partial(per_device, ring=ring), mesh=mesh, in_specs=in_specs, out_specs=out_specs, check_vma=False
    )
```

```python
import functools

import jax
import jax.numpy as jnp
from jax import lax
from jax.experimental import pallas as pl
from jax.experimental.pallas import tpu as pltpu
from jax.sharding import PartitionSpec as P

ITERS = 2
F32 = jnp.float32
BF16 = jnp.bfloat16
NN = (((1,), (0,)), ((), ()))
NT = (((1,), (1,)), ((), ()))


def halves(x):
    high = x.astype(BF16)
    return high, (x - high.astype(F32)).astype(BF16)


def product(a, b, dims=NN):
    a_high, a_low = halves(a)
    b_high, b_low = halves(b)
    dot = functools.partial(lax.dot_general, dimension_numbers=dims, preferred_element_type=F32)
    return dot(a_high, b_high) + (dot(a_high, b_low) + dot(a_low, b_high))


def eye(n):
    return lax.broadcasted_iota(jnp.int32, (n, n), 0) == lax.broadcasted_iota(jnp.int32, (n, n), 1)


def as_row(square):
    column = jnp.sum(square, axis=1, keepdims=True)
    return jnp.sum(jnp.where(eye(square.shape[0]), column, 0.0), axis=0, keepdims=True)


def kernel(
    ring, groups, parts, v_hbm, inj_hbm, cap_hbm, cond_hbm, pat_hbm, gain_hbm, lw_hbm, bvl_hbm, dinv_hbm, bj_hbm, tr_hbm,
    out_ref, v_ref, inj_ref, cap_ref, cond_ref, pat_ref, gain_ref, lw_ref, bvl_ref, dinv_ref, bj_ref, tr_ref, pair2, pair4, pair8, pre, suf, coup, links_t, whole, sufrel, vmat, gwhole, fz, acc,
    before_in, bvl_in, up_in, corr_in, corr, vnext, local, tails, bvec, bsum, share, far, near_sum, far_side, coup2, lead, lead_in,
    load_sem, send_sem, whole_sem, gwhole_sem, bvec_sem, bsum_sem, small_sem, up_sem, corr_sem, far_send, far_sem,
):
    points, nodes = v_ref.shape
    tm, part = lax.axis_index("tm"), lax.axis_index("dom")
    count = ring * groups
    z, g = lax.rem(tm, ring), lax.div(tm, ring)

    def ring_peer(m):
        return g * ring + lax.rem(z + m, ring)

    def group_peer(m):
        return lax.rem(g + m, groups) * ring + z

    loads = {}
    quarter = points // 4
    for k in range(4):
        rows = pl.ds(k * quarter, quarter)
        loads["tr", k] = pltpu.make_async_copy(tr_hbm.at[rows], tr_ref.at[rows], load_sem.at[len(loads)])
        loads["tr", k].start()
    for name, source, target in (
        ("v", v_hbm, v_ref), ("bvl", bvl_hbm, bvl_ref), ("lw", lw_hbm, lw_ref),
        ("bj", bj_hbm, bj_ref), ("dinv", dinv_hbm, dinv_ref), ("inj", inj_hbm, inj_ref), ("cap", cap_hbm, cap_ref),
        ("cond", cond_hbm, cond_ref), ("gain", gain_hbm, gain_ref), ("pat", pat_hbm, pat_ref),
    ):
        loads[name] = pltpu.make_async_copy(source, target, load_sem.at[len(loads)])
        loads[name].start()

    barrier = pltpu.get_barrier_semaphore()
    for m in range(1, ring):
        pl.semaphore_signal(barrier, inc=1, device_id={"tm": ring_peer(m)})
    for m in range(1, groups):
        pl.semaphore_signal(barrier, inc=1, device_id={"tm": group_peer(m)})
    for step in (1, count - 1):
        pl.semaphore_signal(barrier, inc=1, device_id={"tm": lax.rem(tm + step, count)})
    for step in (1, parts - 1):
        pl.semaphore_signal(barrier, inc=1, device_id={"dom": lax.rem(part + step, parts)})

    identity = jnp.where(eye(nodes), 1.0, 0.0)

    for k in range(4):
        loads["tr", k].wait()
        for e in range(k * quarter // 2, (k + 1) * quarter // 2):
            pair2[e] = product(tr_ref[2 * e + 1], tr_ref[2 * e])
    for source, target in ((pair2, pair4), (pair4, pair8)):
        for e in range(target.shape[0]):
            target[e] = product(source[2 * e + 1], source[2 * e])
    whole[0] = product(pair8[1], pair8[0])

    for name in loads:
        if name[0] != "tr":
            loads[name].wait()
    pl.semaphore_wait(barrier, ring - 1 + groups - 1 + 4)

    started = []

    def send(source, target, index, sem, **where):
        copy = pltpu.make_async_remote_copy(
            src_ref=source, dst_ref=target, send_sem=send_sem.at[index], recv_sem=sem,
            device_id=where, device_id_type=pl.DeviceIdType.MESH,
        )
        return copy

    index = iter(range(1000))

    def start(source, target, sem, **where):
        copy = send(source, target, next(index), sem, **where)
        copy.start()
        started.append(copy)
        return copy

    to_next = []

    def start_next(source, target, sem):
        copy = send(source, target, next(index), sem, dom=lax.rem(part + 1, parts))

        @pl.when(part < parts - 1)
        def _():
            copy.start()

        to_next.append(copy)
        return copy

    before_copy = start(v_ref.at[points - 1 :], before_in, small_sem.at[0], tm=lax.rem(tm + 1, count))
    bvl_copy = start_next(bvl_ref, bvl_in, small_sem.at[1])
    up_copies = [start_next(v_ref, up_in.at[0], up_sem.at[0])]
    half = nodes // 2
    top, bottom = pl.ds(0, half), pl.ds(half, half)

    def pass_on(slot, rows, hop, target):
        side = 0 if rows is top else 1
        return start(
            whole.at[slot, rows], whole.at[target, rows], whole_sem.at[target, side], tm=ring_peer(hop)
        )

    whole_copies = {}
    if ring == 8:
        for rows, hop in ((top, 2), (bottom, 6), (bottom, 2), (top, 6), (top, 1), (bottom, 7), (bottom, 1), (top, 7)):
            whole_copies[hop, rows is top] = pass_on(0, rows, hop, hop)
    else:
        for hop in range(1, ring):
            for rows in (top, bottom):
                whole_copies[hop, rows is top] = pass_on(0, rows, hop, hop)

    def forward_ring():
        if ring != 8:
            return
        for slot, rows, last in ((2, top, True), (6, bottom, True), (2, bottom, False), (6, top, False)):
            whole_copies.pop((slot, rows is top)).wait_recv()
            if last:
                whole_copies[4, rows is top] = pass_on(slot, rows, slot, 4)
            side = 1 if slot == 2 else 7
            target = 3 if slot == 2 else 5
            whole_copies[target, rows is top] = pass_on(slot, rows, side, target)

    @pl.when(part > 0)
    def _():
        bvl_copy.wait_recv()
        row = lax.broadcasted_iota(jnp.int32, (nodes, nodes), 0)
        spread = jnp.where(row == bvl_in[...], 1.0, 0.0)
        links_t[...] = product(spread, lw_ref[...], NT)
        acc[0:nodes] = product(bj_ref[...], spread, NT)

        @pl.loop(0, points // 2)
        def _(k):
            for i in range(2):
                coup[2 * k + i] = product(dinv_ref[2 * k + i], acc[0:nodes])

    effective = cond_ref[...] * pat_ref[0].astype(F32)

    def residual(v, before, it):
        r = (
            inj_ref[...]
            - cap_ref[...] * (v - before)
            - product(v, effective, NT)
            - gain_ref[...] * jnp.tanh(v)
        )
        local[...] = r

        @pl.when(part > 0)
        def _():
            up_copies[it].wait_recv()
            local[...] = local[...] + product(up_in[it], links_t[...])

    def suffixes():
        suf[15] = identity
        suf[14] = tr_ref[15]
        suf[13] = pair2[7]
        suf[11] = pair4[3]
        suf[7] = pair8[1]
        suf[9] = product(pair4[3], pair2[5])
        suf[5] = product(pair8[1], pair2[3])
        suf[3] = product(pair8[1], pair4[1])
        suf[1] = product(suf[3], pair2[1])
        for k in range(7):
            suf[2 * k] = product(suf[2 * k + 1], tr_ref[2 * k + 1])

    def act_each(matrices, vectors, store):
        for t in range(points):
            store(t, as_row(matrices[t] * vectors[t : t + 1, :]))

    corr_copies = []
    lead_copy = send(lead, lead_in, next(index), small_sem.at[2], dom=lax.rem(part + 1, parts))
    coup_copy = send(coup, coup2, next(index), small_sem.at[3], dom=lax.rem(part + 1, parts))
    second_copy = send(corr.at[1], corr_in.at[1], next(index), corr_sem.at[1], dom=lax.rem(part + 2, parts))

    @pl.when(part == 2)
    def _():
        coup_copy.start()

    def skip_ahead():
        @pl.when(part == 3)
        def _():
            coup_copy.wait_recv()
            for t in range(points):
                coup2[t] = product(coup[t], coup2[t])

    def correct(it):
        def put(t, row):
            corr[it, pl.ds(t, 1), :] = row

        def add(t, row):
            corr[it, pl.ds(t, 1), :] = corr[it, pl.ds(t, 1), :] + row

        act_each(dinv_ref, local, put)
        corr_copies.append(
            send(corr.at[it], corr_in.at[it], next(index), corr_sem.at[it], dom=lax.rem(part + 1, parts))
        )

        def chain(chosen):
            @pl.when(chosen & (part > 0))
            def _():
                corr_copies[it].wait_recv()
                act_each(coup, corr_in.at[it], add)

            @pl.when(chosen & (part < parts - 1))
            def _():
                corr_copies[it].start()

        if it == 0:
            chain(part < 1)
            forward_ring()
            suffixes()
            chain(part >= 1)
        elif parts != 4:
            chain(part >= 0)
        else:

            @pl.when(part == 2)
            def _():
                lead[...] = corr[it]
                lead_copy.start()

            @pl.when((part == 1) | (part == 2))
            def _():
                corr_copies[it].wait_recv()
                act_each(coup, corr_in.at[it], add)

            @pl.when(part == 3)
            def _():
                lead_copy.wait_recv()
                act_each(coup, lead_in, add)
                corr_copies[it].wait_recv()
                act_each(coup2, corr_in.at[it], add)

            @pl.when(part < 2)
            def _():
                corr_copies[it].start()

            @pl.when(part == 1)
            def _():
                second_copy.start()

        total = suf[0] * corr[it, 0:1, :]
        for t in range(1, points):
            total = total + suf[t] * corr[it, t : t + 1, :]
        bvec[it, 0] = as_row(total)
        return [
            start(bvec.at[it, 0], bvec.at[it, m], bvec_sem.at[it, m], tm=ring_peer(m)) for m in range(1, ring)
        ]

    def sum_local(it):
        def step(t, x):
            x = as_row(tr_ref[t] * x) + corr[it, pl.ds(t, 1), :]
            local[pl.ds(t, 1), :] = x
            return x

        lax.fori_loop(0, points, step, jnp.zeros((1, nodes), F32))

        def put(t, row):
            tails[pl.ds(t, 1), :] = row

        act_each(suf, corr.at[it], put)
        running = jnp.zeros((1, nodes), F32)
        for t in range(points - 1, -1, -1):
            own = tails[t : t + 1, :]
            tails[t : t + 1, :] = running
            running = running + own

    def sum_ring(copies):
        total = sufrel[0] * bvec[0, 0]
        for m in range(1, ring):
            copies[m - 1].wait_recv()
            total = total + sufrel[m] * bvec[0, m]
        bsum[0] = as_row(total)
        return [start(bsum.at[0], bsum.at[m], bsum_sem.at[m], tm=group_peer(m)) for m in range(1, groups)]

    def send_far():
        share[...] = as_row(sufrel[0] * bvec[1, 0])
        ways = sorted(
            ((m, r) for m in range(1, groups) for r in range(ring)),
            key=lambda way: -(min(way[1], ring - way[1]) + min(way[0], groups - way[0]) // 2 + 2 * (way[0] % 2)),
        )
        for m, r in ways:
            pltpu.make_async_remote_copy(
                src_ref=share, dst_ref=far.at[m, pl.ds(r, 1)], send_sem=far_send, recv_sem=far_sem,
                device_id={"tm": lax.rem(g + m, groups) * ring + lax.rem(z + r, ring)},
                device_id_type=pl.DeviceIdType.MESH,
            ).start()

    all_far = pltpu.make_async_remote_copy(
        src_ref=far.at[pl.ds(1, groups - 1)], dst_ref=far.at[pl.ds(1, groups - 1)], send_sem=far_send,
        recv_sem=far_sem, device_id={"tm": ring_peer(1)}, device_id_type=pl.DeviceIdType.MESH,
    )

    def gather_near(it):
        if it > 0:
            for copy in ring_copies[it]:
                copy.wait_recv()
        near = jnp.zeros((nodes, nodes), F32)
        after = jnp.zeros((nodes, nodes), F32)
        for m in range(1, ring):
            behind = m <= z
            term = jnp.where(behind, vmat[m], sufrel[m]) * bvec[it, m]
            near = near + jnp.where(behind, term, 0.0)
            after = after + jnp.where(behind, 0.0, term)
        near_sum[...] = as_row(near)
        own = jnp.concatenate([tails[...], jnp.broadcast_to(bvec[it, 0], (8, nodes))], axis=0)
        far_side[...] = product(own, sufrel[0], NT) + as_row(after)

    def close(it, group_sums, v, store):
        wrapped = product(far_side[...], fz[groups - 1], NT) + near_sum[...]
        near = jnp.zeros((nodes, nodes), F32)
        for m, arrived in enumerate(group_sums(), 1):
            near = near + fz[m - 1] * arrived
        entering = wrapped + as_row(near)
        tails[...] = entering[0:points]

        def put(t, row):
            store(t, v[pl.ds(t, 1), :] + local[pl.ds(t, 1), :] + row)

        act_each(pre, tails, put)
        return entering[points : points + 1]

    v0 = v_ref[...]
    before_copy.wait_recv()
    residual(v0, jnp.concatenate([before_in[...], v0[: points - 1]], axis=0), 0)
    ring_copies = [correct(0)]
    for copy in list(whole_copies.values()):
        copy.wait_recv()

    def ring_slot(j):
        return lax.rem(z - j + ring, ring)

    trees = [whole[ring_slot(j)] for j in range(ring)]
    while len(trees) > 1:
        trees = [product(trees[k + 1], trees[k]) for k in range(0, len(trees), 2)]
    gwhole[0] = trees[0]
    gwhole_copies = [
        start(gwhole.at[0], gwhole.at[m], gwhole_sem.at[m], tm=group_peer(m)) for m in range(1, groups)
    ]
    acc[0:nodes] = identity
    acc[nodes:] = identity

    def ring_step(k, _):
        j = ring - 1 - k
        m = ring_slot(j)
        sufrel[m] = acc[0:nodes]
        vmat[m] = acc[nodes:]
        new = product(acc[...], whole[m])
        acc[0:nodes] = new[0:nodes]
        acc[nodes:] = jnp.where(j < z, new[nodes:], acc[nodes:])
        return 0

    lax.fori_loop(0, ring, ring_step, 0)
    group_copies = sum_ring(ring_copies[0])

    sum_local(0)
    gather_near(0)

    pre[0] = tr_ref[0]
    pre[1] = pair2[0]
    pre[3] = pair4[0]
    pre[7] = pair8[0]
    pre[15] = whole[0]
    pre[5] = product(pair2[2], pair4[0])
    pre[9] = product(pair2[4], pair8[0])
    pre[11] = product(pair4[2], pair8[0])
    pre[13] = product(pair2[6], pre[11])
    for k in range(7):
        pre[2 * k + 2] = product(tr_ref[2 * k + 2], pre[2 * k + 1])

    skip_ahead()

    fz[0] = acc[nodes:]
    for m in range(1, groups):
        gwhole_copies[m - 1].wait_recv()
        fz[m] = product(fz[m - 1], gwhole[m])

    def put_next(t, row):
        vnext[pl.ds(t, 1), :] = row

    def put_out(t, row):
        out_ref[pl.ds(t, 1), :] = row

    def near_sums():
        for m in range(1, groups):
            group_copies[m - 1].wait_recv()
            yield bsum[m]

    def far_sums():
        all_far.wait_recv()
        for m in range(1, groups):
            yield jnp.sum(far[m], axis=0, keepdims=True)

    first = close(0, near_sums, v_ref, put_next)
    up_copies.append(start_next(vnext, up_in.at[1], up_sem.at[1]))

    v1 = vnext[...]
    residual(v1, jnp.concatenate([before_in[...] + first, v1[: points - 1]], axis=0), 1)
    ring_copies.append(correct(1))
    send_far()
    sum_local(1)
    gather_near(1)
    close(1, far_sums, vnext, put_out)
    all_far.wait_send()

    for copy in started:
        copy.wait_send()

    @pl.when(part < parts - 1)
    def _():
        for copy in to_next + corr_copies[:1]:
            copy.wait_send()

    @pl.when(part < (2 if parts == 4 else parts - 1))
    def _():
        corr_copies[1].wait_send()

    @pl.when(part == 1)
    def _():
        if parts == 4:
            second_copy.wait_send()

    @pl.when(part == 2)
    def _():
        lead_copy.wait_send()
        coup_copy.wait_send()


def per_device(
    starting_voltage_guess,
    injected_amperes,
    capacitance,
    conductance,
    block_pattern,
    device_gain,
    link_weight,
    boundary_vertex_list,
    diagonal_reciprocals,
    boundary_jacobian,
    transfer,
    ring,
):
    points, _, nodes = starting_voltage_guess.shape
    count, parts = lax.axis_size("tm"), lax.axis_size("dom")
    groups = count // ring
    square = (nodes, nodes)
    vmem = pl.BlockSpec(memory_space=pltpu.VMEM)
    hbm = pl.BlockSpec(memory_space=pltpu.HBM)
    scratch = [
        pltpu.VMEM((points, nodes), F32),
        pltpu.VMEM((points, nodes), F32),
        pltpu.VMEM((1, nodes), F32),
        pltpu.VMEM(square, F32),
        pltpu.VMEM((1, 1, 1), jnp.int32),
        pltpu.VMEM((1, nodes), F32),
        pltpu.VMEM(square, F32),
        pltpu.VMEM((1, nodes), jnp.int32),
        pltpu.VMEM((points,) + square, F32),
        pltpu.VMEM(square, F32),
        pltpu.VMEM((points,) + square, F32),
        pltpu.VMEM((points // 2,) + square, F32),
        pltpu.VMEM((points // 4,) + square, F32),
        pltpu.VMEM((points // 8,) + square, F32),
        pltpu.VMEM((points,) + square, F32),
        pltpu.VMEM((points,) + square, F32),
        pltpu.VMEM((points,) + square, F32),
        pltpu.VMEM(square, F32),
        pltpu.VMEM((ring,) + square, F32),
        pltpu.VMEM((ring,) + square, F32),
        pltpu.VMEM((ring,) + square, F32),
        pltpu.VMEM((groups,) + square, F32),
        pltpu.VMEM((groups,) + square, F32),
        pltpu.VMEM((2 * nodes, nodes), F32),
        pltpu.VMEM((1, nodes), F32),
        pltpu.VMEM((1, nodes), jnp.int32),
        pltpu.VMEM((ITERS, points, nodes), F32),
        pltpu.VMEM((ITERS, points, nodes), F32),
        pltpu.VMEM((ITERS, points, nodes), F32),
        pltpu.VMEM((points, nodes), F32),
        pltpu.VMEM((points, nodes), F32),
        pltpu.VMEM((points, nodes), F32),
        pltpu.VMEM((ITERS, ring, 1, nodes), F32),
        pltpu.VMEM((groups, 1, nodes), F32),
        pltpu.VMEM((1, nodes), F32),
        pltpu.VMEM((groups, ring, nodes), F32),
        pltpu.VMEM((1, nodes), F32),
        pltpu.VMEM((points + 8, nodes), F32),
        pltpu.VMEM((points,) + square, F32),
        pltpu.VMEM((points, nodes), F32),
        pltpu.VMEM((points, nodes), F32),
        pltpu.SemaphoreType.DMA((14,)),
        pltpu.SemaphoreType.DMA((6 + ITERS * 2 + 4 * (ring + groups),)),
        pltpu.SemaphoreType.DMA((ring, 2)),
        pltpu.SemaphoreType.DMA((groups,)),
        pltpu.SemaphoreType.DMA((ITERS, ring)),
        pltpu.SemaphoreType.DMA((groups,)),
        pltpu.SemaphoreType.DMA((4,)),
        pltpu.SemaphoreType.DMA((ITERS,)),
        pltpu.SemaphoreType.DMA((ITERS,)),
        pltpu.SemaphoreType.DMA,
        pltpu.SemaphoreType.DMA,
    ]
    out = pl.pallas_call(
        functools.partial(kernel, ring, groups, parts),
        out_shape=pltpu.VMEM((points, nodes), F32),
        in_specs=[hbm] * 11,
        out_specs=vmem,
        scratch_shapes=scratch,
        compiler_params=pltpu.CompilerParams(
            collective_id=0, has_side_effects=True, vmem_limit_bytes=66_000_000
        ),
        name="newton",
    )(
        starting_voltage_guess[:, 0],
        injected_amperes[:, 0],
        capacitance,
        conductance[0],
        block_pattern,
        device_gain,
        link_weight[0],
        boundary_vertex_list,
        diagonal_reciprocals[:, 0, 0],
        boundary_jacobian[0],
        transfer[:, 0, 0],
    )
    return out[:, None]


def solution(mesh):
    in_specs = (
        P("tm", "dom", None),
        P("tm", "dom", None),
        P("dom", None),
        P("dom", None, None),
        P("dom", None, None),
        P("dom", None),
        P("dom", None, None),
        P("dom", None),
        P("tm", "dom", None, None, None),
        P("dom", None, None),
        P("tm", "dom", None, None, None),
    )
    out_specs = P("tm", "dom", None)
    count = mesh.shape["tm"]
    ring = 8 if count >= 64 else 2
    return jax.shard_map(
        functools.partial(per_device, ring=ring), mesh=mesh, in_specs=in_specs, out_specs=out_specs, check_vma=False
    )
```

```python
import functools

import jax
import jax.numpy as jnp
from jax import lax
from jax.experimental import pallas as pl
from jax.experimental.pallas import tpu as pltpu
from jax.sharding import PartitionSpec as P

ITERS = 2
F32 = jnp.float32
BF16 = jnp.bfloat16
NN = (((1,), (0,)), ((), ()))
NT = (((1,), (1,)), ((), ()))


def halves(x):
    high = x.astype(BF16)
    return high, (x - high.astype(F32)).astype(BF16)


def product(a, b, dims=NN):
    a_high, a_low = halves(a)
    b_high, b_low = halves(b)
    dot = functools.partial(lax.dot_general, dimension_numbers=dims, preferred_element_type=F32)
    return dot(a_high, b_high) + (dot(a_high, b_low) + dot(a_low, b_high))


def eye(n):
    return lax.broadcasted_iota(jnp.int32, (n, n), 0) == lax.broadcasted_iota(jnp.int32, (n, n), 1)


def as_row(square):
    column = jnp.sum(square, axis=1, keepdims=True)
    return jnp.sum(jnp.where(eye(square.shape[0]), column, 0.0), axis=0, keepdims=True)


def kernel(
    ring, groups, parts, v_hbm, inj_hbm, cap_hbm, cond_hbm, pat_hbm, gain_hbm, lw_hbm, bvl_hbm, dinv_hbm, bj_hbm, tr_hbm,
    out_ref, v_ref, inj_ref, cap_ref, cond_ref, pat_ref, gain_ref, lw_ref, bvl_ref, dinv_ref, bj_ref, tr_ref, pair2, pair4, pair8, pre, suf, coup, links_t, whole, sufrel, vmat, gwhole, fz, acc,
    before_in, bvl_in, up_in, corr_in, corr, vnext, local, tails, bvec, bsum, share, far, near_sum, far_side, coup2, lead, lead_in,
    load_sem, send_sem, whole_sem, gwhole_sem, bvec_sem, bsum_sem, small_sem, up_sem, corr_sem, far_send, far_sem,
):
    points, nodes = v_ref.shape
    tm, part = lax.axis_index("tm"), lax.axis_index("dom")
    count = ring * groups
    z, g = lax.rem(tm, ring), lax.div(tm, ring)

    def ring_peer(m):
        return g * ring + lax.rem(z + m, ring)

    def group_peer(m):
        return lax.rem(g + m, groups) * ring + z

    loads = {}
    quarter = points // 4
    for k in range(4):
        rows = pl.ds(k * quarter, quarter)
        loads["tr", k] = pltpu.make_async_copy(tr_hbm.at[rows], tr_ref.at[rows], load_sem.at[len(loads)])
        loads["tr", k].start()
    for name, source, target in (
        ("v", v_hbm, v_ref), ("bvl", bvl_hbm, bvl_ref), ("lw", lw_hbm, lw_ref),
        ("bj", bj_hbm, bj_ref), ("dinv", dinv_hbm, dinv_ref), ("inj", inj_hbm, inj_ref), ("cap", cap_hbm, cap_ref),
        ("cond", cond_hbm, cond_ref), ("gain", gain_hbm, gain_ref), ("pat", pat_hbm, pat_ref),
    ):
        loads[name] = pltpu.make_async_copy(source, target, load_sem.at[len(loads)])
        loads[name].start()

    barrier = pltpu.get_barrier_semaphore()
    for m in range(1, ring):
        pl.semaphore_signal(barrier, inc=1, device_id={"tm": ring_peer(m)})
    for m in range(1, groups):
        pl.semaphore_signal(barrier, inc=1, device_id={"tm": group_peer(m)})
    for step in (1, count - 1):
        pl.semaphore_signal(barrier, inc=1, device_id={"tm": lax.rem(tm + step, count)})
    for step in (1, parts - 1):
        pl.semaphore_signal(barrier, inc=1, device_id={"dom": lax.rem(part + step, parts)})

    identity = jnp.where(eye(nodes), 1.0, 0.0)

    for k in range(4):
        loads["tr", k].wait()
        for e in range(k * quarter // 2, (k + 1) * quarter // 2):
            pair2[e] = product(tr_ref[2 * e + 1], tr_ref[2 * e])
    for source, target in ((pair2, pair4), (pair4, pair8)):
        for e in range(target.shape[0]):
            target[e] = product(source[2 * e + 1], source[2 * e])
    whole[0] = product(pair8[1], pair8[0])

    for name in loads:
        if name[0] != "tr":
            loads[name].wait()
    pl.semaphore_wait(barrier, ring - 1 + groups - 1 + 4)

    started = []

    def send(source, target, index, sem, **where):
        copy = pltpu.make_async_remote_copy(
            src_ref=source, dst_ref=target, send_sem=send_sem.at[index], recv_sem=sem,
            device_id=where, device_id_type=pl.DeviceIdType.MESH,
        )
        return copy

    index = iter(range(1000))

    def start(source, target, sem, **where):
        copy = send(source, target, next(index), sem, **where)
        copy.start()
        started.append(copy)
        return copy

    to_next = []

    def start_next(source, target, sem):
        copy = send(source, target, next(index), sem, dom=lax.rem(part + 1, parts))

        @pl.when(part < parts - 1)
        def _():
            copy.start()

        to_next.append(copy)
        return copy

    before_copy = start(v_ref.at[points - 1 :], before_in, small_sem.at[0], tm=lax.rem(tm + 1, count))
    bvl_copy = start_next(bvl_ref, bvl_in, small_sem.at[1])
    up_copies = [start_next(v_ref, up_in.at[0], up_sem.at[0])]
    half = nodes // 2
    top, bottom = pl.ds(0, half), pl.ds(half, half)

    def pass_on(slot, rows, hop, target):
        side = 0 if rows is top else 1
        return start(
            whole.at[slot, rows], whole.at[target, rows], whole_sem.at[target, side], tm=ring_peer(hop)
        )

    whole_copies = {}
    if ring == 8:
        for rows, hop in ((top, 2), (bottom, 6), (top, 1), (bottom, 7), (bottom, 2), (top, 6), (bottom, 1), (top, 7)):
            whole_copies[hop, rows is top] = pass_on(0, rows, hop, hop)
    else:
        for hop in range(1, ring):
            for rows in (top, bottom):
                whole_copies[hop, rows is top] = pass_on(0, rows, hop, hop)

    def forward_ring():
        if ring != 8:
            return
        for slot, rows, last in ((2, top, True), (6, bottom, True), (2, bottom, False), (6, top, False)):
            whole_copies.pop((slot, rows is top)).wait_recv()
            if last:
                whole_copies[4, rows is top] = pass_on(slot, rows, slot, 4)
            side = 1 if slot == 2 else 7
            target = 3 if slot == 2 else 5
            whole_copies[target, rows is top] = pass_on(slot, rows, side, target)

    @pl.when(part > 0)
    def _():
        bvl_copy.wait_recv()
        row = lax.broadcasted_iota(jnp.int32, (nodes, nodes), 0)
        spread = jnp.where(row == bvl_in[...], 1.0, 0.0)
        links_t[...] = product(spread, lw_ref[...], NT)
        acc[0:nodes] = product(bj_ref[...], spread, NT)

        @pl.loop(0, points // 2)
        def _(k):
            for i in range(2):
                coup[2 * k + i] = product(dinv_ref[2 * k + i], acc[0:nodes])

    effective = cond_ref[...] * pat_ref[0].astype(F32)

    def residual(v, before, it):
        r = (
            inj_ref[...]
            - cap_ref[...] * (v - before)
            - product(v, effective, NT)
            - gain_ref[...] * jnp.tanh(v)
        )
        local[...] = r

        @pl.when(part > 0)
        def _():
            up_copies[it].wait_recv()
            local[...] = local[...] + product(up_in[it], links_t[...])

    def suffixes():
        suf[15] = identity
        suf[14] = tr_ref[15]
        suf[13] = pair2[7]
        suf[11] = pair4[3]
        suf[7] = pair8[1]
        suf[9] = product(pair4[3], pair2[5])
        suf[5] = product(pair8[1], pair2[3])
        suf[3] = product(pair8[1], pair4[1])
        suf[1] = product(suf[3], pair2[1])
        for k in range(7):
            suf[2 * k] = product(suf[2 * k + 1], tr_ref[2 * k + 1])

    def act_each(matrices, vectors, store):
        for t in range(points):
            store(t, as_row(matrices[t] * vectors[t : t + 1, :]))

    corr_copies = []
    lead_copy = send(lead, lead_in, next(index), small_sem.at[2], dom=lax.rem(part + 1, parts))
    coup_copy = send(coup, coup2, next(index), small_sem.at[3], dom=lax.rem(part + 1, parts))
    second_copy = send(corr.at[1], corr_in.at[1], next(index), corr_sem.at[1], dom=lax.rem(part + 2, parts))

    @pl.when(part == 2)
    def _():
        coup_copy.start()

    def skip_ahead():
        @pl.when(part == 3)
        def _():
            coup_copy.wait_recv()
            for t in range(points):
                coup2[t] = product(coup[t], coup2[t])

    def correct(it):
        def put(t, row):
            corr[it, pl.ds(t, 1), :] = row

        def add(t, row):
            corr[it, pl.ds(t, 1), :] = corr[it, pl.ds(t, 1), :] + row

        act_each(dinv_ref, local, put)
        corr_copies.append(
            send(corr.at[it], corr_in.at[it], next(index), corr_sem.at[it], dom=lax.rem(part + 1, parts))
        )

        def chain(chosen):
            @pl.when(chosen & (part > 0))
            def _():
                corr_copies[it].wait_recv()
                act_each(coup, corr_in.at[it], add)

            @pl.when(chosen & (part < parts - 1))
            def _():
                corr_copies[it].start()

        if it == 0:
            chain(part < 1)
            forward_ring()
            suffixes()
            chain(part >= 1)
        elif parts != 4:
            chain(part >= 0)
        else:

            @pl.when(part == 2)
            def _():
                lead[...] = corr[it]
                lead_copy.start()

            @pl.when((part == 1) | (part == 2))
            def _():
                corr_copies[it].wait_recv()
                act_each(coup, corr_in.at[it], add)

            @pl.when(part == 3)
            def _():
                lead_copy.wait_recv()
                act_each(coup, lead_in, add)
                corr_copies[it].wait_recv()
                act_each(coup2, corr_in.at[it], add)

            @pl.when(part < 2)
            def _():
                corr_copies[it].start()

            @pl.when(part == 1)
            def _():
                second_copy.start()

        total = suf[0] * corr[it, 0:1, :]
        for t in range(1, points):
            total = total + suf[t] * corr[it, t : t + 1, :]
        bvec[it, 0] = as_row(total)
        return [
            start(bvec.at[it, 0], bvec.at[it, m], bvec_sem.at[it, m], tm=ring_peer(m)) for m in range(1, ring)
        ]

    def sum_local(it):
        def step(t, x):
            x = as_row(tr_ref[t] * x) + corr[it, pl.ds(t, 1), :]
            local[pl.ds(t, 1), :] = x
            return x

        lax.fori_loop(0, points, step, jnp.zeros((1, nodes), F32))

        def put(t, row):
            tails[pl.ds(t, 1), :] = row

        act_each(suf, corr.at[it], put)
        running = jnp.zeros((1, nodes), F32)
        for t in range(points - 1, -1, -1):
            own = tails[t : t + 1, :]
            tails[t : t + 1, :] = running
            running = running + own

    def sum_ring(copies):
        total = sufrel[0] * bvec[0, 0]
        for m in range(1, ring):
            copies[m - 1].wait_recv()
            total = total + sufrel[m] * bvec[0, m]
        bsum[0] = as_row(total)
        return [start(bsum.at[0], bsum.at[m], bsum_sem.at[m], tm=group_peer(m)) for m in range(1, groups)]

    def send_far():
        share[...] = as_row(sufrel[0] * bvec[1, 0])
        ways = sorted(
            ((m, r) for m in range(1, groups) for r in range(ring)),
            key=lambda way: -(min(way[1], ring - way[1]) + min(way[0], groups - way[0]) // 2 + 2 * (way[0] % 2)),
        )
        for m, r in ways:
            pltpu.make_async_remote_copy(
                src_ref=share, dst_ref=far.at[m, pl.ds(r, 1)], send_sem=far_send, recv_sem=far_sem,
                device_id={"tm": lax.rem(g + m, groups) * ring + lax.rem(z + r, ring)},
                device_id_type=pl.DeviceIdType.MESH,
            ).start()

    all_far = pltpu.make_async_remote_copy(
        src_ref=far.at[pl.ds(1, groups - 1)], dst_ref=far.at[pl.ds(1, groups - 1)], send_sem=far_send,
        recv_sem=far_sem, device_id={"tm": ring_peer(1)}, device_id_type=pl.DeviceIdType.MESH,
    )

    def gather_near(it):
        if it > 0:
            for copy in ring_copies[it]:
                copy.wait_recv()
        near = jnp.zeros((nodes, nodes), F32)
        after = jnp.zeros((nodes, nodes), F32)
        for m in range(1, ring):
            behind = m <= z
            term = jnp.where(behind, vmat[m], sufrel[m]) * bvec[it, m]
            near = near + jnp.where(behind, term, 0.0)
            after = after + jnp.where(behind, 0.0, term)
        near_sum[...] = as_row(near)
        own = jnp.concatenate([tails[...], jnp.broadcast_to(bvec[it, 0], (8, nodes))], axis=0)
        far_side[...] = product(own, sufrel[0], NT) + as_row(after)

    def close(it, group_sums, v, store):
        wrapped = product(far_side[...], fz[groups - 1], NT) + near_sum[...]
        near = jnp.zeros((nodes, nodes), F32)
        for m, arrived in enumerate(group_sums(), 1):
            near = near + fz[m - 1] * arrived
        entering = wrapped + as_row(near)
        tails[...] = entering[0:points]

        def put(t, row):
            store(t, v[pl.ds(t, 1), :] + local[pl.ds(t, 1), :] + row)

        act_each(pre, tails, put)
        return entering[points : points + 1]

    v0 = v_ref[...]
    before_copy.wait_recv()
    residual(v0, jnp.concatenate([before_in[...], v0[: points - 1]], axis=0), 0)
    ring_copies = [correct(0)]
    for copy in list(whole_copies.values()):
        copy.wait_recv()

    def ring_slot(j):
        return lax.rem(z - j + ring, ring)

    trees = [whole[ring_slot(j)] for j in range(ring)]
    while len(trees) > 1:
        trees = [product(trees[k + 1], trees[k]) for k in range(0, len(trees), 2)]
    gwhole[0] = trees[0]
    gwhole_copies = [
        start(gwhole.at[0], gwhole.at[m], gwhole_sem.at[m], tm=group_peer(m)) for m in range(1, groups)
    ]
    acc[0:nodes] = identity
    acc[nodes:] = identity

    def ring_step(k, _):
        j = ring - 1 - k
        m = ring_slot(j)
        sufrel[m] = acc[0:nodes]
        vmat[m] = acc[nodes:]
        new = product(acc[...], whole[m])
        acc[0:nodes] = new[0:nodes]
        acc[nodes:] = jnp.where(j < z, new[nodes:], acc[nodes:])
        return 0

    lax.fori_loop(0, ring, ring_step, 0)
    group_copies = sum_ring(ring_copies[0])

    sum_local(0)
    gather_near(0)

    pre[0] = tr_ref[0]
    pre[1] = pair2[0]
    pre[3] = pair4[0]
    pre[7] = pair8[0]
    pre[15] = whole[0]
    pre[5] = product(pair2[2], pair4[0])
    pre[9] = product(pair2[4], pair8[0])
    pre[11] = product(pair4[2], pair8[0])
    pre[13] = product(pair2[6], pre[11])
    for k in range(7):
        pre[2 * k + 2] = product(tr_ref[2 * k + 2], pre[2 * k + 1])

    skip_ahead()

    fz[0] = acc[nodes:]
    for m in range(1, groups):
        gwhole_copies[m - 1].wait_recv()
        fz[m] = product(fz[m - 1], gwhole[m])

    def put_next(t, row):
        vnext[pl.ds(t, 1), :] = row

    def put_out(t, row):
        out_ref[pl.ds(t, 1), :] = row

    def near_sums():
        for m in range(1, groups):
            group_copies[m - 1].wait_recv()
            yield bsum[m]

    def far_sums():
        all_far.wait_recv()
        for m in range(1, groups):
            yield jnp.sum(far[m], axis=0, keepdims=True)

    first = close(0, near_sums, v_ref, put_next)
    up_copies.append(start_next(vnext, up_in.at[1], up_sem.at[1]))

    v1 = vnext[...]
    residual(v1, jnp.concatenate([before_in[...] + first, v1[: points - 1]], axis=0), 1)
    ring_copies.append(correct(1))
    send_far()
    sum_local(1)
    gather_near(1)
    close(1, far_sums, vnext, put_out)
    all_far.wait_send()

    for copy in started:
        copy.wait_send()

    @pl.when(part < parts - 1)
    def _():
        for copy in to_next + corr_copies[:1]:
            copy.wait_send()

    @pl.when(part < (2 if parts == 4 else parts - 1))
    def _():
        corr_copies[1].wait_send()

    @pl.when(part == 1)
    def _():
        if parts == 4:
            second_copy.wait_send()

    @pl.when(part == 2)
    def _():
        lead_copy.wait_send()
        coup_copy.wait_send()


def per_device(
    starting_voltage_guess,
    injected_amperes,
    capacitance,
    conductance,
    block_pattern,
    device_gain,
    link_weight,
    boundary_vertex_list,
    diagonal_reciprocals,
    boundary_jacobian,
    transfer,
    ring,
):
    points, _, nodes = starting_voltage_guess.shape
    count, parts = lax.axis_size("tm"), lax.axis_size("dom")
    groups = count // ring
    square = (nodes, nodes)
    vmem = pl.BlockSpec(memory_space=pltpu.VMEM)
    hbm = pl.BlockSpec(memory_space=pltpu.HBM)
    scratch = [
        pltpu.VMEM((points, nodes), F32),
        pltpu.VMEM((points, nodes), F32),
        pltpu.VMEM((1, nodes), F32),
        pltpu.VMEM(square, F32),
        pltpu.VMEM((1, 1, 1), jnp.int32),
        pltpu.VMEM((1, nodes), F32),
        pltpu.VMEM(square, F32),
        pltpu.VMEM((1, nodes), jnp.int32),
        pltpu.VMEM((points,) + square, F32),
        pltpu.VMEM(square, F32),
        pltpu.VMEM((points,) + square, F32),
        pltpu.VMEM((points // 2,) + square, F32),
        pltpu.VMEM((points // 4,) + square, F32),
        pltpu.VMEM((points // 8,) + square, F32),
        pltpu.VMEM((points,) + square, F32),
        pltpu.VMEM((points,) + square, F32),
        pltpu.VMEM((points,) + square, F32),
        pltpu.VMEM(square, F32),
        pltpu.VMEM((ring,) + square, F32),
        pltpu.VMEM((ring,) + square, F32),
        pltpu.VMEM((ring,) + square, F32),
        pltpu.VMEM((groups,) + square, F32),
        pltpu.VMEM((groups,) + square, F32),
        pltpu.VMEM((2 * nodes, nodes), F32),
        pltpu.VMEM((1, nodes), F32),
        pltpu.VMEM((1, nodes), jnp.int32),
        pltpu.VMEM((ITERS, points, nodes), F32),
        pltpu.VMEM((ITERS, points, nodes), F32),
        pltpu.VMEM((ITERS, points, nodes), F32),
        pltpu.VMEM((points, nodes), F32),
        pltpu.VMEM((points, nodes), F32),
        pltpu.VMEM((points, nodes), F32),
        pltpu.VMEM((ITERS, ring, 1, nodes), F32),
        pltpu.VMEM((groups, 1, nodes), F32),
        pltpu.VMEM((1, nodes), F32),
        pltpu.VMEM((groups, ring, nodes), F32),
        pltpu.VMEM((1, nodes), F32),
        pltpu.VMEM((points + 8, nodes), F32),
        pltpu.VMEM((points,) + square, F32),
        pltpu.VMEM((points, nodes), F32),
        pltpu.VMEM((points, nodes), F32),
        pltpu.SemaphoreType.DMA((14,)),
        pltpu.SemaphoreType.DMA((6 + ITERS * 2 + 4 * (ring + groups),)),
        pltpu.SemaphoreType.DMA((ring, 2)),
        pltpu.SemaphoreType.DMA((groups,)),
        pltpu.SemaphoreType.DMA((ITERS, ring)),
        pltpu.SemaphoreType.DMA((groups,)),
        pltpu.SemaphoreType.DMA((4,)),
        pltpu.SemaphoreType.DMA((ITERS,)),
        pltpu.SemaphoreType.DMA((ITERS,)),
        pltpu.SemaphoreType.DMA,
        pltpu.SemaphoreType.DMA,
    ]
    out = pl.pallas_call(
        functools.partial(kernel, ring, groups, parts),
        out_shape=pltpu.VMEM((points, nodes), F32),
        in_specs=[hbm] * 11,
        out_specs=vmem,
        scratch_shapes=scratch,
        compiler_params=pltpu.CompilerParams(
            collective_id=0, has_side_effects=True, vmem_limit_bytes=66_000_000
        ),
        name="newton",
    )(
        starting_voltage_guess[:, 0],
        injected_amperes[:, 0],
        capacitance,
        conductance[0],
        block_pattern,
        device_gain,
        link_weight[0],
        boundary_vertex_list,
        diagonal_reciprocals[:, 0, 0],
        boundary_jacobian[0],
        transfer[:, 0, 0],
    )
    return out[:, None]


def solution(mesh):
    in_specs = (
        P("tm", "dom", None),
        P("tm", "dom", None),
        P("dom", None),
        P("dom", None, None),
        P("dom", None, None),
        P("dom", None),
        P("dom", None, None),
        P("dom", None),
        P("tm", "dom", None, None, None),
        P("dom", None, None),
        P("tm", "dom", None, None, None),
    )
    out_specs = P("tm", "dom", None)
    count = mesh.shape["tm"]
    ring = 8 if count >= 64 else 2
    return jax.shard_map(
        functools.partial(per_device, ring=ring), mesh=mesh, in_specs=in_specs, out_specs=out_specs, check_vma=False
    )
```
